128 devices in a mesh: section: 4 (over z), mp: 32 (over y, x, core).
Axes of the slice: x: 4, y: 4, z: 4, core: 2. Of those that a mesh axis runs over, the one named last changes fastest.
Arguments:
- entering_hidden: bfloat16 [4, 256, 8192], P('section', None, 'mp'), may hold values from -12 to 12
- section_weight: bfloat16 [4, 8192, 8192], P('section', None, 'mp'), may hold values from -0.0625 to 0.0625
- section_norm_gain: bfloat16 [4, 8192], P('section', 'mp'), may hold values from 0.5 to 1.5
- plugin_narrowing_factors: bfloat16 [4, 32, 8192, 64], P('section', 'mp'), may hold values from -0.0625 to 0.0625
- plugin_widening_factors: bfloat16 [4, 32, 64, 8192], P('section', 'mp'), may hold values from -0.75 to 0.75
- reward_head: bfloat16 [8192], P('mp'), may hold values from -0.0625 to 0.0625
- adapter_of_block: int32 [4, 2], replicated, may hold values from 0 to 31
- live_block_rows: int32 [4, 2], P('section'), may hold values from 1 to 128
Outputs:
- hidden_out: bfloat16 [4, 256, 8192], P('section', None, 'mp')
- scores: float32 [4, 256], P('section')
The draws below stay inside these ranges and needn't reach their ends.
All inputs are finite; a program needn't handle non-finite values.
Results may differ from the reference program's by a relative error of at most 0.022.
Values may be sent and summed in bfloat16 or wider, within the bound.
A program may use at most 64 MiB of HBM per device.

```python
import math
import jax
import jax.numpy as jnp
import numpy as np
from jax import lax

EMBED_DIMENSION = 8192
FACTOR_DIMENSION = 64
BLOCK = 128
BLK_MB = 2
PLUGIN_TOTAL = 32
MICRO = 4
ROWS_MB = 256
N_SECTION = 4


def draw_entering_hidden(key, part):
    first_key = jax.random.fold_in(key, 0)
    column = jnp.arange(EMBED_DIMENSION, dtype=jnp.float32) / EMBED_DIMENSION
    rising = 0.5 * jnp.exp(column * math.log(3.0))
    values = jnp.clip(jax.random.normal(first_key, (MICRO, ROWS_MB, EMBED_DIMENSION), jnp.float32), -4.0, 4.0)
    return jnp.clip(values * rising[None, None, :], -12.0, 12.0).astype(jnp.bfloat16)


def set_ends(entries, key, low, largest):
    extent = entries.shape
    index_at = [jax.random.randint(jax.random.fold_in(key, axis), (), 0, extent[axis]) for axis in range(len(extent))]
    entries = entries.at[tuple(index_at)].set(low)
    longest = extent.index(max(extent))
    index_at[longest] = (index_at[longest] + 1) % extent[longest]
    return entries.at[tuple(index_at)].set(largest)


def steps_of(own_key, shape, cuts, smallest, high):
    level, own = 1.0, jax.random.fold_in(own_key, 6)
    for position, parts in cuts:
        heights = jnp.exp(jax.random.uniform(jax.random.fold_in(own, position), (parts,), jnp.float32, smallest / len(cuts), high / len(cuts)))
        level = level * jnp.repeat(heights, shape[position] // parts).reshape([-1 if axis == position else 1 for axis in range(len(shape))])
    return level


def cumulative_ranks(amount, slope):
    loads = [(1 << 20) // math.isqrt(rank ** slope) + 1 for rank in range(1, amount + 1)]
    scale = 1 + sum(loads) // (1 << 30)
    return np.cumsum(np.array([max(1, weight // scale) for weight in loads]))


def ranked_ids(key, extent, amount, slope):
    grid = cumulative_ranks(amount, slope)
    lot = jax.random.randint(jax.random.fold_in(key, 1), extent, 0, int(grid[amount - 1]))
    standing = jnp.searchsorted(jnp.asarray(grid, jnp.int32), lot, side="right")
    return jax.random.permutation(jax.random.fold_in(key, 2), amount)[standing].astype(jnp.int32)


def centred(key, dims, scale, most, cuts=(), kind=jnp.bfloat16):
    result = jax.random.normal(key, dims, jnp.float32) * scale
    if len(cuts) > 0:
        result = steps_of(key, dims, cuts, -0.22, 0.18) * result
    return jnp.clip(result, min=-most, max=most).astype(kind)


def setup_inputs(seed: int = 0) -> dict:
    streams_of = jax.random.split(jax.random.key(seed), 9)
    return {
        "entering_hidden": draw_entering_hidden(jax.random.fold_in(streams_of[8], 71), 0),
        "section_weight": centred(streams_of[1], (N_SECTION, EMBED_DIMENSION, EMBED_DIMENSION), EMBED_DIMENSION ** -0.5, 0.0625, ((0, 4), (2, 32))),
        "section_norm_gain": jnp.clip(1.0 + 0.1 * jax.random.normal(streams_of[2], (N_SECTION, EMBED_DIMENSION), jnp.float32), 0.5, 1.5).astype(jnp.bfloat16),
        "plugin_narrowing_factors": centred(streams_of[3], (N_SECTION, PLUGIN_TOTAL, EMBED_DIMENSION, FACTOR_DIMENSION), EMBED_DIMENSION ** -0.5, 0.0625, ((0, 4), (1, 32))),
        "plugin_widening_factors": centred(streams_of[4], (N_SECTION, PLUGIN_TOTAL, FACTOR_DIMENSION, EMBED_DIMENSION), FACTOR_DIMENSION ** -0.5, 0.75, ((0, 4), (1, 32))),
        "reward_head": centred(streams_of[5], (EMBED_DIMENSION,), EMBED_DIMENSION ** -0.5, 0.0625, ((0, 32),)),
        "adapter_of_block": set_ends(ranked_ids(streams_of[6], (MICRO, BLK_MB), PLUGIN_TOTAL, 2), jax.random.fold_in(streams_of[6], 3), 0, PLUGIN_TOTAL - 1).astype(jnp.int32),
        "live_block_rows": set_ends(jax.random.randint(streams_of[7], (MICRO, BLK_MB), 1, BLOCK + 1), jax.random.fold_in(streams_of[7], 1), 1, BLOCK).astype(jnp.int32),
    }


def layer_of_section(hidden_state, weight, gain, down_maps, up_maps, adapter_numbers):
    hidden_f = hidden_state.astype(jnp.float32)
    squares = lax.optimization_barrier(jnp.sum(hidden_f * hidden_f, axis=1, keepdims=True))
    rescaled_activation = (hidden_f * lax.rsqrt(squares / EMBED_DIMENSION + 1e-05) * gain.astype(jnp.float32)).astype(jnp.bfloat16)
    base = jnp.dot(rescaled_activation.astype(jnp.float32), weight.astype(jnp.float32), preferred_element_type=jnp.float32, precision=lax.Precision.HIGHEST)
    blocks = rescaled_activation.reshape(-1, BLOCK, EMBED_DIMENSION).astype(jnp.float32)
    chosen_down = down_maps[adapter_numbers].astype(jnp.float32)
    compressed_projection = jnp.einsum('brd,bdk->brk', blocks, chosen_down, precision=lax.Precision.HIGHEST).astype(jnp.bfloat16)
    chosen_expansion_matrix = up_maps[adapter_numbers].astype(jnp.float32)
    thin_correction = jnp.einsum('sin,sny->siy', compressed_projection.astype(jnp.float32), chosen_expansion_matrix, precision=lax.Precision.HIGHEST).reshape(-1, EMBED_DIMENSION)
    return (hidden_f + base + 2.0 * thin_correction).astype(jnp.bfloat16)

def reference(entering_hidden, section_weight, section_norm_gain, plugin_narrowing_factors, plugin_widening_factors, reward_head, adapter_of_block, live_block_rows):
    hidden_state = entering_hidden.reshape(MICRO * ROWS_MB, EMBED_DIMENSION)
    adapter_numbers = adapter_of_block.reshape(-1)
    for section_ordinal in range(N_SECTION):
        hidden_state = layer_of_section(hidden_state, section_weight[section_ordinal], section_norm_gain[section_ordinal], plugin_narrowing_factors[section_ordinal], plugin_widening_factors[section_ordinal], adapter_numbers)
    hidden_out = hidden_state.reshape(MICRO, ROWS_MB, EMBED_DIMENSION)
    raw = lax.optimization_barrier(jnp.sum(hidden_out.astype(jnp.float32) * reward_head.astype(jnp.float32), axis=2))
    place = jnp.arange(ROWS_MB, dtype=jnp.int32) % BLOCK
    limits = jnp.repeat(live_block_rows, BLOCK, axis=1)
    scores = jnp.where(place[None, :] < limits, raw, jnp.float32(0.0))
    return (hidden_out, scores)
```

```python
import functools

import jax
import jax.numpy as jnp
from jax import lax
from jax.experimental import pallas as pl
from jax.experimental.pallas import tpu as pltpu
from jax.sharding import PartitionSpec as P

MESH = pl.DeviceIdType.MESH
BLOCK = 128
CHUNK = 64
COLOURS = 4
STEPS = 4
PIECE = CHUNK // COLOURS
RING = 4
WIDTH = 256
RANK = 64
LANES = 128

A, B, C, D = (1, 0), (3, 0), (0, 1), (0, 3)
ORDER = ((A, B, C, D), (B, A, D, C), (C, D, A, B), (D, C, B, A))


def flipped(position, mask):
    if mask == 0:
        return position
    if mask == 1:
        return position + 1 - 2 * lax.rem(position, 2)
    if mask == 2:
        return lax.rem(position + 2, 4)
    return 3 - position


def slots():
    tables = []
    for order in ORDER:
        table = {}
        for slot in range(2**STEPS):
            bits_x, bits_y = 0, 0
            for step in range(STEPS):
                if slot >> step & 1:
                    bits_x ^= order[step][0]
                    bits_y ^= order[step][1]
            table[bits_y * 4 + bits_x] = slot
        tables.append(table)
    return tables


SLOT = slots()


def encode(value, lane):
    high = value.astype(jnp.bfloat16).astype(jnp.float32)
    low = pltpu.roll(value - high, 1, axis=1)
    return jnp.where(lane == RANK + 1, low, value).astype(jnp.bfloat16)


def decode(message, lane):
    value = message.astype(jnp.float32)
    low = pltpu.roll(value, LANES - 1, axis=1)
    value = jnp.where(lane == RANK, value + low, value)
    return jnp.where(lane == RANK + 1, 0.0, value)


def kernel(
    chunks,
    adapter_ref,
    live_ref,
    enter_ref,
    weight_ref,
    gain_ref,
    narrow_ref,
    widen_ref,
    head_ref,
    out_ref,
    score_ref,
    hz,
    gathered,
    sums_out,
    sums_in,
    running,
    final_sums,
    sib_sums,
    part_out,
    part_in,
    own_part,
    next_h,
    w_own,
    w_sib,
    narrow_v,
    packed,
    narrow_t,
    widen_t,
    finished,
    score_part,
    score_all,
    gs,
    gr,
    as_,
    ar_,
    xs,
    xr,
    zs,
    zr,
    fs,
    fr,
    once,
):
    section = lax.axis_index("section")
    mp = lax.axis_index("mp")
    core = lax.rem(mp, 2)
    chip = lax.div(mp, 2)
    x = lax.rem(chip, RING)
    y = lax.div(chip, RING)
    other = mp + 1 - 2 * core
    per_micro = 256 // CHUNK

    def mesh_id(where, rank):
        return {"section": where, "mp": rank}

    barrier = pltpu.get_barrier_semaphore()
    for offset in range(1, 32):
        pl.semaphore_signal(
            barrier, inc=1, device_id=mesh_id(section, lax.rem(mp + offset, 32)), device_id_type=MESH
        )
    for offset in range(1, 4):
        pl.semaphore_signal(
            barrier, inc=1, device_id=mesh_id(lax.rem(section + offset, 4), mp), device_id_type=MESH
        )

    narrow_load = pltpu.make_async_copy(narrow_ref, narrow_v, once.at[0])
    narrow_load.start()

    def chip_of(rel):
        return flipped(y, rel // 4) * RING + flipped(x, rel % 4)

    for rel in range(16):
        rows = pl.ds(pl.multiple_of((chip_of(rel) * 2 + core) * WIDTH, WIDTH), WIDTH)
        pltpu.make_async_copy(
            weight_ref.at[rows], w_own.at[pl.ds(rel * WIDTH, WIDTH)], once.at[1]
        ).start()

    @pl.when(section == 0)
    def _():
        for part in range(per_micro):
            pltpu.make_async_copy(
                enter_ref.at[pl.ds(part * CHUNK, CHUNK)], hz.at[part], zr.at[part]
            ).start()

    pl.semaphore_wait(barrier, 34)

    @pl.when(section > 0)
    def _():
        for part in range(per_micro):
            index = section * per_micro + part
            pltpu.make_async_remote_copy(
                src_ref=enter_ref.at[pl.ds(part * CHUNK, CHUNK)],
                dst_ref=hz.at[index],
                send_sem=fs.at[part],
                recv_sem=zr.at[index],
                device_id=mesh_id(0, mp),
                device_id_type=MESH,
            ).start()

    def swap_weight(rel):
        rows = pl.ds(pl.multiple_of((chip_of(rel) * 2 + 1 - core) * WIDTH, WIDTH), WIDTH)
        return pltpu.make_async_remote_copy(
            src_ref=weight_ref.at[rows],
            dst_ref=w_sib.at[pl.ds(rel * WIDTH, WIDTH)],
            send_sem=once.at[2],
            recv_sem=once.at[3],
            device_id=mesh_id(section, other),
            device_id_type=MESH,
        )

    for rel in range(16):
        swap_weight(rel).start()

    def widen_send(offset):
        target = lax.rem(mp + offset, 32)
        return pltpu.make_async_remote_copy(
            src_ref=widen_ref.at[:, pl.ds(pl.multiple_of(target * WIDTH, WIDTH), WIDTH)],
            dst_ref=widen_t.at[mp],
            send_sem=once.at[4],
            recv_sem=once.at[5],
            device_id=mesh_id(section, target),
            device_id_type=MESH,
        )

    def narrow_send(offset):
        target = lax.rem(mp + offset, 32)
        return pltpu.make_async_remote_copy(
            src_ref=packed.at[target],
            dst_ref=narrow_t.at[mp],
            send_sem=once.at[6],
            recv_sem=once.at[7],
            device_id=mesh_id(section, target),
            device_id_type=MESH,
        )

    narrow_load.wait()

    @pl.loop(0, 32)
    def _(target):
        tile = narrow_v[pl.ds(pl.multiple_of(target * WIDTH, WIDTH), WIDTH), :]
        packed[target] = jnp.concatenate([tile[:128], tile[128:]], axis=1)

    @pl.loop(1, 32)
    def _(offset):
        narrow_send(offset).start()
        widen_send(offset).start()

    pltpu.make_async_copy(packed.at[mp], narrow_t.at[mp], once.at[7]).start()
    pltpu.make_async_copy(
        widen_ref.at[:, pl.ds(pl.multiple_of(mp * WIDTH, WIDTH), WIDTH)], widen_t.at[mp], once.at[5]
    ).start()

    lane = lax.broadcasted_iota(jnp.int32, (CHUNK, LANES), 1)
    gain = gain_ref[...].astype(jnp.float32)

    def adapter_of(index):
        return adapter_ref[lax.div(index, per_micro), lax.div(lax.rem(index, per_micro), BLOCK // CHUNK)]

    def step_copies(index, step):
        ring_slot = lax.rem(index, 4)
        copies = []
        for colour in range(COLOURS):
            mask_x, mask_y = ORDER[colour][step]
            partner = (flipped(y, mask_y) * RING + flipped(x, mask_x)) * 2 + core
            count = 2**step
            copies.append(
                pltpu.make_async_remote_copy(
                    src_ref=gathered.at[index, colour, pl.ds(0, count)],
                    dst_ref=gathered.at[index, colour, pl.ds(count, count)],
                    send_sem=gs.at[ring_slot, step, colour],
                    recv_sem=gr.at[ring_slot, step, colour],
                    device_id=mesh_id(section, partner),
                    device_id_type=MESH,
                )
            )
            rows = pl.ds(colour * PIECE, PIECE)
            copies.append(
                pltpu.make_async_remote_copy(
                    src_ref=sums_out.at[index, step, rows],
                    dst_ref=sums_in.at[index, step, rows],
                    send_sem=as_.at[ring_slot, step, colour],
                    recv_sem=ar_.at[ring_slot, step, colour],
                    device_id=mesh_id(section, partner),
                    device_id_type=MESH,
                )
            )
        return copies

    def start_step(index, step):
        for copy in step_copies(index, step):
            copy.start()

    def finish_step(index, step):
        for copy in step_copies(index, step):
            copy.wait()
        total = running[index] + decode(sums_in[index, step], lane)
        if step < STEPS - 1:
            running[index] = total
            sums_out[index, step + 1] = encode(total, lane)
        else:
            final_sums[index] = total

    def prepare(index):
        pltpu.make_async_copy(hz.at[index], hz.at[index], zr.at[index]).wait()
        h = hz[index].astype(jnp.float32)
        squares = jnp.sum(h * h, axis=1, keepdims=True)
        scaled = (h * gain).astype(jnp.bfloat16)
        for colour in range(COLOURS):
            gathered[index, colour, 0] = scaled[colour * PIECE : (colour + 1) * PIECE]
        maps = narrow_t[adapter_of(index)]
        first = jnp.dot(scaled[:, :128], maps, preferred_element_type=jnp.float32)
        second = jnp.dot(scaled[:, 128:], maps, preferred_element_type=jnp.float32)
        inner = first + pltpu.roll(second, RANK, axis=1)
        value = jnp.where(lane < RANK, inner, jnp.where(lane == RANK, squares, 0.0))
        running[index] = value
        sums_out[index, 0] = encode(value, lane)
        start_step(index, 0)

    def left_side(index):
        return jnp.concatenate(
            [
                jnp.concatenate([gathered[index, colour, SLOT[colour][rel]] for colour in range(COLOURS)], axis=0)
                for rel in range(16)
            ],
            axis=1,
        )

    def swaps(index):
        ring_slot = lax.rem(index, 4)
        sums = pltpu.make_async_remote_copy(
            src_ref=final_sums.at[index],
            dst_ref=sib_sums.at[index],
            send_sem=xs.at[ring_slot, 0],
            recv_sem=xr.at[ring_slot, 0],
            device_id=mesh_id(section, other),
            device_id_type=MESH,
        )
        parts = pltpu.make_async_remote_copy(
            src_ref=part_out.at[index],
            dst_ref=part_in.at[index],
            send_sem=xs.at[ring_slot, 1],
            recv_sem=xr.at[ring_slot, 1],
            device_id=mesh_id(section, other),
            device_id_type=MESH,
        )
        return sums, parts

    def multiply_sibling(index):
        sums, parts = swaps(index)
        sums.start()
        part_out[index] = jnp.dot(left_side(index), w_sib[...], preferred_element_type=jnp.float32)
        parts.start()

    def multiply_own(index):
        own_part[...] = jnp.dot(left_side(index), w_own[...], preferred_element_type=jnp.float32)

    def onward(index):
        return pltpu.make_async_remote_copy(
            src_ref=next_h.at[index],
            dst_ref=hz.at[index],
            send_sem=zs.at[index],
            recv_sem=zr.at[index],
            device_id=mesh_id(lax.rem(section + 1, 4), mp),
            device_id_type=MESH,
        )

    def homeward(index):
        home = lax.div(index, per_micro)
        part = lax.rem(index, per_micro)
        return pltpu.make_async_remote_copy(
            src_ref=next_h.at[index],
            dst_ref=finished.at[part],
            send_sem=zs.at[index],
            recv_sem=fr.at[part],
            device_id=mesh_id(home, mp),
            device_id_type=MESH,
        )

    def combine(index):
        sums, parts = swaps(index)
        sums.wait()
        parts.wait()
        total = final_sums[index] + sib_sums[index]
        squares = jnp.sum(jnp.where(lane == RANK, total, 0.0), axis=1, keepdims=True)
        scale = lax.rsqrt(squares / (WIDTH * 32) + 1e-05)
        inner = total[:, :RANK].astype(jnp.bfloat16)
        delta = jnp.dot(inner, widen_t[adapter_of(index)], preferred_element_type=jnp.float32)
        base = own_part[...] + part_in[index]
        h = hz[index].astype(jnp.float32)
        next_h[index] = (h + scale * (base + 2.0 * delta)).astype(jnp.bfloat16)

        @pl.when(section < 3)
        def _():
            onward(index).start()

        @pl.when(section == 3)
        def _():
            @pl.when(index < 3 * per_micro)
            def _():
                homeward(index).start()

            @pl.when(index >= 3 * per_micro)
            def _():
                part = lax.rem(index, per_micro)
                pltpu.make_async_copy(next_h.at[index], finished.at[part], fr.at[part]).start()

    pltpu.make_async_copy(narrow_t, narrow_t, once.at[7]).wait()
    pltpu.make_async_copy(widen_t, widen_t, once.at[5]).wait()
    pltpu.make_async_copy(w_own, w_own, once.at[1]).wait()
    pltpu.make_async_copy(w_sib, w_sib, once.at[3]).wait()
    pltpu.make_async_copy(w_sib, w_sib, once.at[2]).wait()
    pltpu.make_async_copy(narrow_t.at[pl.ds(0, 31)], narrow_t.at[pl.ds(0, 31)], once.at[6]).wait()
    pltpu.make_async_copy(widen_t.at[pl.ds(0, 31)], widen_t.at[pl.ds(0, 31)], once.at[4]).wait()

    @pl.loop(0, chunks + 2)
    def _(tick):
        @pl.when((tick >= 1) & (tick <= chunks))
        def _():
            finish_step(tick - 1, 2)
            start_step(tick - 1, 3)

        @pl.when(tick < chunks)
        def _():
            prepare(tick)

        @pl.when(tick >= 2)
        def _():
            finish_step(tick - 2, 3)
            multiply_sibling(tick - 2)

        @pl.when(tick < chunks)
        def _():
            finish_step(tick, 0)
            start_step(tick, 1)

        @pl.when(tick >= 2)
        def _():
            multiply_own(tick - 2)
            combine(tick - 2)

        @pl.when(tick < chunks)
        def _():
            finish_step(tick, 1)
            start_step(tick, 2)

    @pl.when(section > 0)
    def _():
        for part in range(per_micro):
            pltpu.make_async_copy(hz.at[0], hz.at[0], fs.at[part]).wait()

    @pl.loop(0, chunks)
    def _(index):
        @pl.when((section < 3) | (index < 3 * per_micro))
        def _():
            pltpu.make_async_copy(next_h.at[index], next_h.at[index], zs.at[index]).wait()

    for part in range(per_micro):
        pltpu.make_async_copy(finished.at[part], finished.at[part], fr.at[part]).wait()
    hidden = jnp.concatenate([finished[part] for part in range(per_micro)], axis=0)
    out_ref[...] = hidden
    head = jnp.broadcast_to(head_ref[...], (8, WIDTH))
    partial = lax.dot_general(head, hidden, (((1,), (1,)), ((), ())), preferred_element_type=jnp.float32)
    score_part[...] = partial[:1]

    def score_send(offset):
        return pltpu.make_async_remote_copy(
            src_ref=score_part,
            dst_ref=score_all.at[mp],
            send_sem=once.at[8],
            recv_sem=once.at[9],
            device_id=mesh_id(section, lax.rem(mp + offset, 32)),
            device_id_type=MESH,
        )

    @pl.loop(1, 32)
    def _(offset):
        score_send(offset).start()

    pltpu.make_async_copy(score_part, score_all.at[mp], once.at[9]).start()
    pltpu.make_async_copy(score_all, score_all, once.at[9]).wait()
    pltpu.make_async_copy(score_all.at[pl.ds(0, 31)], score_all.at[pl.ds(0, 31)], once.at[8]).wait()
    raw = jnp.sum(score_all[...], axis=0)
    place = lax.broadcasted_iota(jnp.int32, (1, 2 * BLOCK), 1)
    limit = jnp.where(place < BLOCK, live_ref[0, 0], live_ref[0, 1])
    score_ref[...] = jnp.where(lax.rem(place, BLOCK) < limit, raw, 0.0)


def shards(
    entering_hidden,
    section_weight,
    section_norm_gain,
    plugin_narrowing_factors,
    plugin_widening_factors,
    reward_head,
    adapter_of_block,
    live_block_rows,
):
    chunks = 1024 // CHUNK
    bf16, f32 = jnp.bfloat16, jnp.float32
    vmem = pl.BlockSpec(memory_space=pltpu.VMEM)
    smem = pl.BlockSpec(memory_space=pltpu.SMEM)
    anywhere = pl.BlockSpec(memory_space=pl.ANY)
    dma = pltpu.SemaphoreType.DMA
    hidden, scores = pl.pallas_call(
        functools.partial(kernel, chunks),
        out_shape=(
            jax.ShapeDtypeStruct((256, WIDTH), bf16),
            jax.ShapeDtypeStruct((1, 256), f32),
        ),
        in_specs=[smem, smem, anywhere, anywhere, vmem, anywhere, anywhere, vmem],
        out_specs=(vmem, vmem),
        scratch_shapes=[
            pltpu.VMEM((chunks, CHUNK, WIDTH), bf16),
            pltpu.VMEM((chunks, COLOURS, 16, PIECE, WIDTH), bf16),
            pltpu.VMEM((chunks, STEPS, CHUNK, LANES), bf16),
            pltpu.VMEM((chunks, STEPS, CHUNK, LANES), bf16),
            pltpu.VMEM((chunks, CHUNK, LANES), f32),
            pltpu.VMEM((chunks, CHUNK, LANES), f32),
            pltpu.VMEM((chunks, CHUNK, LANES), f32),
            pltpu.VMEM((chunks, CHUNK, WIDTH), f32),
            pltpu.VMEM((chunks, CHUNK, WIDTH), f32),
            pltpu.VMEM((CHUNK, WIDTH), f32),
            pltpu.VMEM((chunks, CHUNK, WIDTH), bf16),
            pltpu.VMEM((16 * WIDTH, WIDTH), bf16),
            pltpu.VMEM((16 * WIDTH, WIDTH), bf16),
            pltpu.VMEM((32 * WIDTH, RANK), bf16),
            pltpu.VMEM((32, 128, LANES), bf16),
            pltpu.VMEM((32, 128, LANES), bf16),
            pltpu.VMEM((32, RANK, WIDTH), bf16),
            pltpu.VMEM((256 // CHUNK, CHUNK, WIDTH), bf16),
            pltpu.VMEM((1, 256), f32),
            pltpu.VMEM((32, 1, 256), f32),
            dma((4, STEPS, COLOURS)),
            dma((4, STEPS, COLOURS)),
            dma((4, STEPS, COLOURS)),
            dma((4, STEPS, COLOURS)),
            dma((4, 2)),
            dma((4, 2)),
            dma((chunks,)),
            dma((chunks,)),
            dma((4,)),
            dma((4,)),
            dma((10,)),
        ],
        compiler_params=pltpu.CompilerParams(
            collective_id=0, has_side_effects=True, vmem_limit_bytes=60 * 1024 * 1024
        ),
    )(
        adapter_of_block,
        live_block_rows,
        entering_hidden[0],
        section_weight[0],
        section_norm_gain,
        plugin_narrowing_factors[0, 0],
        plugin_widening_factors[0, 0],
        reward_head[None, :],
    )
    return hidden[None], scores


def solution(mesh):
    placed = (
        P("section", None, "mp"),
        P("section", None, "mp"),
        P("section", "mp"),
        P("section", "mp", None, None),
        P("section", "mp", None, None),
        P("mp"),
        P(),
        P("section", None),
    )
    return jax.shard_map(
        shards,
        mesh=mesh,
        in_specs=placed,
        out_specs=(P("section", None, "mp"), P("section", None)),
        check_vma=False,
    )
```

```python
import functools

import jax
import jax.numpy as jnp
from jax import lax
from jax.experimental import pallas as pl
from jax.experimental.pallas import tpu as pltpu
from jax.sharding import PartitionSpec as P

MESH = pl.DeviceIdType.MESH
BLOCK = 128
CHUNK = 64
COLOURS = 2
PHASES = 2
PIECE = CHUNK // COLOURS
RING = 4
WIDTH = 256
RANK = 64
LANES = 128
RETIRE = 3

FAR = ((2, 2), (3, 2), (2, 3), (1, 2), (2, 1), (0, 2), (2, 0), (3, 1), (1, 3), (3, 3), (1, 1), (0, 3), (3, 0), (0, 1), (1, 0))


def flipped(position, mask):
    if mask == 0:
        return position
    if mask == 1:
        return position + 1 - 2 * lax.rem(position, 2)
    if mask == 2:
        return lax.rem(position + 2, 4)
    return 3 - position


def slot_of(colour, rel):
    return (rel // 4, rel % 4) if colour == 0 else (rel % 4, rel // 4)


def encode(value, lane):
    high = value.astype(jnp.bfloat16).astype(jnp.float32)
    low = pltpu.roll(value - high, 1, axis=1)
    return jnp.where(lane == RANK + 1, low, value).astype(jnp.bfloat16)


def decode(message, lane):
    value = message.astype(jnp.float32)
    low = pltpu.roll(value, LANES - 1, axis=1)
    value = jnp.where(lane == RANK, value + low, value)
    return jnp.where(lane == RANK + 1, 0.0, value)


def kernel(
    chunks,
    adapter_ref,
    live_ref,
    enter_ref,
    weight_ref,
    gain_ref,
    narrow_ref,
    widen_ref,
    head_ref,
    out_ref,
    score_ref,
    hz,
    gathered,
    sums_out,
    sums_in,
    running,
    final_sums,
    sib_sums,
    part_out,
    part_in,
    own_part,
    next_h,
    w_own,
    w_sib,
    narrow_t,
    widen_t,
    finished,
    score_part,
    score_all,
    gs,
    gr,
    as_,
    ar_,
    xs,
    xr,
    zs,
    zr,
    fs,
    fr,
    once,
):
    section = lax.axis_index("section")
    mp = lax.axis_index("mp")
    core = lax.rem(mp, 2)
    chip = lax.div(mp, 2)
    x = lax.rem(chip, RING)
    y = lax.div(chip, RING)
    other = mp + 1 - 2 * core
    per_micro = 256 // CHUNK

    def mesh_id(where, rank):
        return {"section": where, "mp": rank}

    barrier = pltpu.get_barrier_semaphore()
    for offset in range(1, 32):
        pl.semaphore_signal(
            barrier, inc=1, device_id=mesh_id(section, lax.rem(mp + offset, 32)), device_id_type=MESH
        )
    for offset in range(1, 4):
        pl.semaphore_signal(
            barrier, inc=1, device_id=mesh_id(lax.rem(section + offset, 4), mp), device_id_type=MESH
        )

    def chip_of(rel):
        return flipped(y, rel // 4) * RING + flipped(x, rel % 4)

    for rel in range(16):
        rows = pl.ds(pl.multiple_of((chip_of(rel) * 2 + core) * WIDTH, WIDTH), WIDTH)
        pltpu.make_async_copy(
            weight_ref.at[rows], w_own.at[pl.ds(rel * WIDTH, WIDTH)], once.at[1]
        ).start()

    @pl.when(section == 0)
    def _():
        for part in range(per_micro):
            pltpu.make_async_copy(
                enter_ref.at[pl.ds(part * CHUNK, CHUNK)], hz.at[part], zr.at[part]
            ).start()

    pl.semaphore_wait(barrier, 34)

    @pl.when(section > 0)
    def _():
        for part in range(per_micro):
            index = section * per_micro + part
            pltpu.make_async_remote_copy(
                src_ref=enter_ref.at[pl.ds(part * CHUNK, CHUNK)],
                dst_ref=hz.at[index],
                send_sem=fs.at[part],
                recv_sem=zr.at[index],
                device_id=mesh_id(0, mp),
                device_id_type=MESH,
            ).start()

    def swap_weight(rel):
        rows = pl.ds(pl.multiple_of((chip_of(rel) * 2 + 1 - core) * WIDTH, WIDTH), WIDTH)
        return pltpu.make_async_remote_copy(
            src_ref=weight_ref.at[rows],
            dst_ref=w_sib.at[pl.ds(rel * WIDTH, WIDTH)],
            send_sem=once.at[2],
            recv_sem=once.at[3],
            device_id=mesh_id(section, other),
            device_id_type=MESH,
        )

    def columns(rank):
        return pl.ds(pl.multiple_of(rank * WIDTH, WIDTH), WIDTH)

    def spread(source, table, send, receive):
        for other_core in (0, 1):
            for mask_x, mask_y in FAR + (((0, 0),) if other_core else ()):
                rank = (flipped(y, mask_y) * RING + flipped(x, mask_x)) * 2 + (1 - core if other_core else core)
                pltpu.make_async_remote_copy(
                    src_ref=source.at[:, columns(rank)],
                    dst_ref=table.at[mp],
                    send_sem=once.at[send],
                    recv_sem=once.at[receive],
                    device_id=mesh_id(section, rank),
                    device_id_type=MESH,
                ).start()
        pltpu.make_async_copy(source.at[:, columns(mp)], table.at[mp], once.at[receive]).start()

    spread(narrow_ref, narrow_t, 6, 7)
    for rel in range(16):
        swap_weight(rel).start()
    spread(widen_ref, widen_t, 4, 5)

    lane = lax.broadcasted_iota(jnp.int32, (CHUNK, LANES), 1)
    gain = gain_ref[...].astype(jnp.float32)

    def adapter_of(index):
        return adapter_ref[lax.div(index, per_micro), lax.div(lax.rem(index, per_micro), BLOCK // CHUNK)]

    def phase_copies(index, phase):
        ring_slot = lax.rem(index, 4)
        copies = []
        for mask in (2, 3, 1):
            for colour in range(COLOURS):
                mask_x, mask_y = (mask, 0) if colour == phase else (0, mask)
                partner = (flipped(y, mask_y) * RING + flipped(x, mask_x)) * 2 + core
                piece = gathered.at[index, colour]
                rows = pl.ds(colour * PIECE, PIECE)
                copies.append(
                    pltpu.make_async_remote_copy(
                        src_ref=piece.at[0, 0] if phase == 0 else piece.at[0],
                        dst_ref=piece.at[0, mask] if phase == 0 else piece.at[mask],
                        send_sem=gs.at[ring_slot, phase, colour, mask - 1],
                        recv_sem=gr.at[ring_slot, phase, colour, mask - 1],
                        device_id=mesh_id(section, partner),
                        device_id_type=MESH,
                    )
                )
                copies.append(
                    pltpu.make_async_remote_copy(
                        src_ref=sums_out.at[index, phase, rows],
                        dst_ref=sums_in.at[index, phase, mask - 1, rows],
                        send_sem=as_.at[ring_slot, phase, colour, mask - 1],
                        recv_sem=ar_.at[ring_slot, phase, colour, mask - 1],
                        device_id=mesh_id(section, partner),
                        device_id_type=MESH,
                    )
                )
        return copies

    def start_phase(index, phase):
        for copy in phase_copies(index, phase):
            copy.start()

    def finish_phase(index, phase):
        for copy in phase_copies(index, phase):
            copy.wait_recv()
        total = running[index]
        for peer in range(3):
            total = total + decode(sums_in[index, phase, peer], lane)
        if phase == 0:
            running[index] = total
            sums_out[index, 1] = encode(total, lane)
        else:
            final_sums[index] = total

    def prepare(index):
        pltpu.make_async_copy(hz.at[index], hz.at[index], zr.at[index]).wait()
        h = hz[index].astype(jnp.float32)
        squares = jnp.sum(h * h, axis=1, keepdims=True)
        scaled = (h * gain).astype(jnp.bfloat16)
        for colour in range(COLOURS):
            gathered[index, colour, 0, 0] = scaled[colour * PIECE : (colour + 1) * PIECE]
        inner = lax.dot_general(
            scaled, narrow_t[adapter_of(index)], (((1,), (1,)), ((), ())), preferred_element_type=jnp.float32
        )
        half_lane = lax.broadcasted_iota(jnp.int32, (CHUNK, LANES - RANK), 1)
        value = jnp.concatenate([inner, jnp.where(half_lane == 0, squares, 0.0)], axis=1)
        running[index] = value
        sums_out[index, 0] = encode(value, lane)
        start_phase(index, 0)

    def left_side(index):
        return jnp.concatenate(
            [
                jnp.concatenate([gathered[(index, colour) + slot_of(colour, rel)] for colour in range(COLOURS)], axis=0)
                for rel in range(16)
            ],
            axis=1,
        )

    def swaps(index):
        ring_slot = lax.rem(index, 4)
        sums = pltpu.make_async_remote_copy(
            src_ref=final_sums.at[index],
            dst_ref=sib_sums.at[index],
            send_sem=xs.at[ring_slot, 0],
            recv_sem=xr.at[ring_slot, 0],
            device_id=mesh_id(section, other),
            device_id_type=MESH,
        )
        parts = pltpu.make_async_remote_copy(
            src_ref=part_out.at[index],
            dst_ref=part_in.at[index],
            send_sem=xs.at[ring_slot, 1],
            recv_sem=xr.at[ring_slot, 1],
            device_id=mesh_id(section, other),
            device_id_type=MESH,
        )
        return sums, parts

    def multiply_sibling(index):
        sums, parts = swaps(index)
        sums.start()
        part_out[index] = jnp.dot(left_side(index), w_sib[...], preferred_element_type=jnp.float32)
        parts.start()

    def multiply_own(index):
        own_part[...] = jnp.dot(left_side(index), w_own[...], preferred_element_type=jnp.float32)

    def onward(index):
        return pltpu.make_async_remote_copy(
            src_ref=next_h.at[index],
            dst_ref=hz.at[index],
            send_sem=zs.at[index],
            recv_sem=zr.at[index],
            device_id=mesh_id(lax.rem(section + 1, 4), mp),
            device_id_type=MESH,
        )

    def homeward(index):
        home = lax.div(index, per_micro)
        part = lax.rem(index, per_micro)
        return pltpu.make_async_remote_copy(
            src_ref=next_h.at[index],
            dst_ref=finished.at[part],
            send_sem=zs.at[index],
            recv_sem=fr.at[part],
            device_id=mesh_id(home, mp),
            device_id_type=MESH,
        )

    def combine(index):
        sums, parts = swaps(index)
        sums.wait_recv()
        parts.wait_recv()
        total = final_sums[index] + sib_sums[index]
        squares = jnp.sum(jnp.where(lane == RANK, total, 0.0), axis=1, keepdims=True)
        scale = lax.rsqrt(squares / (WIDTH * 32) + 1e-05)
        inner = total[:, :RANK].astype(jnp.bfloat16)
        delta = jnp.dot(inner, widen_t[adapter_of(index)], preferred_element_type=jnp.float32)
        base = own_part[...] + part_in[index]
        h = hz[index].astype(jnp.float32)
        next_h[index] = (h + scale * (base + 2.0 * delta)).astype(jnp.bfloat16)

        @pl.when(section < 3)
        def _():
            onward(index).start()

        @pl.when(section == 3)
        def _():
            @pl.when(index < 3 * per_micro)
            def _():
                homeward(index).start()

            @pl.when(index >= 3 * per_micro)
            def _():
                part = lax.rem(index, per_micro)
                pltpu.make_async_copy(next_h.at[index], finished.at[part], fr.at[part]).start()

    def retire(index):
        for phase in range(PHASES):
            for copy in phase_copies(index, phase):
                copy.wait_send()
        for copy in swaps(index):
            copy.wait_send()

    pltpu.make_async_copy(narrow_t, narrow_t, once.at[7]).wait()

    @pl.loop(0, chunks + RETIRE)
    def _(tick):
        @pl.when(tick < chunks)
        def _():
            prepare(tick)

        @pl.when((tick >= 1) & (tick <= chunks))
        def _():
            finish_phase(tick - 1, 0)
            start_phase(tick - 1, 1)

        @pl.when(tick == 2)
        def _():
            pltpu.make_async_copy(w_own, w_own, once.at[1]).wait()
            pltpu.make_async_copy(w_sib, w_sib, once.at[3]).wait()
            pltpu.make_async_copy(w_sib, w_sib, once.at[2]).wait()
            pltpu.make_async_copy(narrow_t.at[pl.ds(0, 31)], narrow_t.at[pl.ds(0, 31)], once.at[6]).wait()
            pltpu.make_async_copy(widen_t, widen_t, once.at[5]).wait()
            pltpu.make_async_copy(widen_t.at[pl.ds(0, 31)], widen_t.at[pl.ds(0, 31)], once.at[4]).wait()

        @pl.when((tick >= 2) & (tick <= chunks + 1))
        def _():
            finish_phase(tick - 2, 1)
            multiply_sibling(tick - 2)
            multiply_own(tick - 2)
            combine(tick - 2)

        @pl.when(tick >= RETIRE)
        def _():
            retire(tick - RETIRE)

    @pl.when(section > 0)
    def _():
        for part in range(per_micro):
            pltpu.make_async_copy(hz.at[0], hz.at[0], fs.at[part]).wait()

    @pl.loop(0, chunks)
    def _(index):
        @pl.when((section < 3) | (index < 3 * per_micro))
        def _():
            pltpu.make_async_copy(next_h.at[index], next_h.at[index], zs.at[index]).wait()

    for part in range(per_micro):
        pltpu.make_async_copy(finished.at[part], finished.at[part], fr.at[part]).wait()
    hidden = jnp.concatenate([finished[part] for part in range(per_micro)], axis=0)
    out_ref[...] = hidden
    head = jnp.broadcast_to(head_ref[...], (8, WIDTH))
    partial = lax.dot_general(head, hidden, (((1,), (1,)), ((), ())), preferred_element_type=jnp.float32)
    score_part[...] = partial[:1]

    def score_send(offset):
        return pltpu.make_async_remote_copy(
            src_ref=score_part,
            dst_ref=score_all.at[mp],
            send_sem=once.at[8],
            recv_sem=once.at[9],
            device_id=mesh_id(section, lax.rem(mp + offset, 32)),
            device_id_type=MESH,
        )

    @pl.loop(1, 32)
    def _(offset):
        score_send(offset).start()

    pltpu.make_async_copy(score_part, score_all.at[mp], once.at[9]).start()
    pltpu.make_async_copy(score_all, score_all, once.at[9]).wait()
    pltpu.make_async_copy(score_all.at[pl.ds(0, 31)], score_all.at[pl.ds(0, 31)], once.at[8]).wait()
    raw = jnp.sum(score_all[...], axis=0)
    place = lax.broadcasted_iota(jnp.int32, (1, 2 * BLOCK), 1)
    limit = jnp.where(place < BLOCK, live_ref[0, 0], live_ref[0, 1])
    score_ref[...] = jnp.where(lax.rem(place, BLOCK) < limit, raw, 0.0)


def shards(
    entering_hidden,
    section_weight,
    section_norm_gain,
    plugin_narrowing_factors,
    plugin_widening_factors,
    reward_head,
    adapter_of_block,
    live_block_rows,
):
    chunks = 1024 // CHUNK
    bf16, f32 = jnp.bfloat16, jnp.float32
    vmem = pl.BlockSpec(memory_space=pltpu.VMEM)
    smem = pl.BlockSpec(memory_space=pltpu.SMEM)
    anywhere = pl.BlockSpec(memory_space=pl.ANY)
    dma = pltpu.SemaphoreType.DMA
    hidden, scores = pl.pallas_call(
        functools.partial(kernel, chunks),
        out_shape=(
            jax.ShapeDtypeStruct((256, WIDTH), bf16),
            jax.ShapeDtypeStruct((1, 256), f32),
        ),
        in_specs=[smem, smem, anywhere, anywhere, vmem, anywhere, anywhere, vmem],
        out_specs=(vmem, vmem),
        scratch_shapes=[
            pltpu.VMEM((chunks, CHUNK, WIDTH), bf16),
            pltpu.VMEM((chunks, COLOURS, RING, RING, PIECE, WIDTH), bf16),
            pltpu.VMEM((chunks, PHASES, CHUNK, LANES), bf16),
            pltpu.VMEM((chunks, PHASES, 3, CHUNK, LANES), bf16),
            pltpu.VMEM((chunks, CHUNK, LANES), f32),
            pltpu.VMEM((chunks, CHUNK, LANES), f32),
            pltpu.VMEM((chunks, CHUNK, LANES), f32),
            pltpu.VMEM((chunks, CHUNK, WIDTH), f32),
            pltpu.VMEM((chunks, CHUNK, WIDTH), f32),
            pltpu.VMEM((CHUNK, WIDTH), f32),
            pltpu.VMEM((chunks, CHUNK, WIDTH), bf16),
            pltpu.VMEM((16 * WIDTH, WIDTH), bf16),
            pltpu.VMEM((16 * WIDTH, WIDTH), bf16),
            pltpu.VMEM((32, RANK, WIDTH), bf16),
            pltpu.VMEM((32, RANK, WIDTH), bf16),
            pltpu.VMEM((256 // CHUNK, CHUNK, WIDTH), bf16),
            pltpu.VMEM((1, 256), f32),
            pltpu.VMEM((32, 1, 256), f32),
            dma((4, PHASES, COLOURS, 3)),
            dma((4, PHASES, COLOURS, 3)),
            dma((4, PHASES, COLOURS, 3)),
            dma((4, PHASES, COLOURS, 3)),
            dma((4, 2)),
            dma((4, 2)),
            dma((chunks,)),
            dma((chunks,)),
            dma((4,)),
            dma((4,)),
            dma((10,)),
        ],
        compiler_params=pltpu.CompilerParams(
            collective_id=0, has_side_effects=True, vmem_limit_bytes=60 * 1024 * 1024
        ),
    )(
        adapter_of_block,
        live_block_rows,
        entering_hidden[0],
        section_weight[0],
        section_norm_gain,
        plugin_narrowing_factors[0, 0].T,
        plugin_widening_factors[0, 0],
        reward_head[None, :],
    )
    return hidden[None], scores


def solution(mesh):
    placed = (
        P("section", None, "mp"),
        P("section", None, "mp"),
        P("section", "mp"),
        P("section", "mp", None, None),
        P("section", "mp", None, None),
        P("mp"),
        P(),
        P("section", None),
    )
    return jax.shard_map(
        shards,
        mesh=mesh,
        in_specs=placed,
        out_specs=(P("section", None, "mp"), P("section", None)),
        check_vma=False,
    )
```

```python
import functools

import jax
import jax.numpy as jnp
from jax import lax
from jax.experimental import pallas as pl
from jax.experimental.pallas import tpu as pltpu
from jax.sharding import PartitionSpec as P

MESH = pl.DeviceIdType.MESH
BLOCK = 128
CHUNK = 64
COLOURS = 2
PHASES = 2
PIECE = CHUNK // COLOURS
RING = 4
WIDTH = 256
RANK = 64
LANES = 128
LATE = 3
RETIRE = 4
DEPTH = 5

FAR = ((2, 2), (3, 2), (2, 3), (1, 2), (2, 1), (0, 2), (2, 0), (3, 1), (1, 3), (3, 3), (1, 1), (0, 3), (3, 0), (0, 1), (1, 0))


def flipped(position, mask):
    if mask == 0:
        return position
    if mask == 1:
        return position + 1 - 2 * lax.rem(position, 2)
    if mask == 2:
        return lax.rem(position + 2, 4)
    return 3 - position


def slot_of(colour, rel):
    return (rel // 4, rel % 4) if colour == 0 else (rel % 4, rel // 4)


def pack(value):
    pieces = []
    for colour in range(COLOURS):
        first = colour * PIECE
        pieces.append(
            jnp.concatenate([value[first : first + PIECE // 2], value[first + PIECE // 2 : first + PIECE]], axis=1)
        )
    return jnp.concatenate(pieces, axis=0)


def unpack(value):
    pieces = []
    for colour in range(COLOURS):
        piece = value[colour * PIECE // 2 : (colour + 1) * PIECE // 2]
        pieces += [piece[:, :RANK], piece[:, RANK:]]
    return jnp.concatenate(pieces, axis=0)


def kernel(
    chunks,
    adapter_ref,
    live_ref,
    enter_ref,
    weight_ref,
    gain_ref,
    narrow_ref,
    widen_ref,
    head_ref,
    out_ref,
    score_ref,
    gathered,
    sums_out,
    sums_in,
    running,
    final_sums,
    sib_sums,
    part_out,
    part_in,
    own_part,
    next_h,
    w_own,
    w_sib,
    narrow_t,
    widen_t,
    gain_o,
    gains,
    finished,
    score_part,
    score_all,
    gs,
    gr,
    as_,
    ar_,
    xs,
    xr,
    zs,
    zo,
    zr,
    fs,
    fr,
    once,
):
    section = lax.axis_index("section")
    mp = lax.axis_index("mp")
    core = lax.rem(mp, 2)
    chip = lax.div(mp, 2)
    x = lax.rem(chip, RING)
    y = lax.div(chip, RING)
    other = mp + 1 - 2 * core
    per_micro = 256 // CHUNK

    def mesh_id(where, rank):
        return {"section": where, "mp": rank}

    barrier = pltpu.get_barrier_semaphore()
    for offset in range(1, 32):
        pl.semaphore_signal(
            barrier, inc=1, device_id=mesh_id(section, lax.rem(mp + offset, 32)), device_id_type=MESH
        )
    for offset in range(1, 4):
        pl.semaphore_signal(
            barrier, inc=1, device_id=mesh_id(lax.rem(section + offset, 4), mp), device_id_type=MESH
        )

    def chip_of(rel):
        return flipped(y, rel // 4) * RING + flipped(x, rel % 4)

    for rel in range(16):
        rows = pl.ds(pl.multiple_of((chip_of(rel) * 2 + core) * WIDTH, WIDTH), WIDTH)
        pltpu.make_async_copy(
            weight_ref.at[rows], w_own.at[pl.ds(rel * WIDTH, WIDTH)], once.at[1]
        ).start()

    @pl.when(section == 0)
    def _():
        for part in range(per_micro):
            for colour in range(COLOURS):
                pltpu.make_async_copy(
                    enter_ref.at[pl.ds(part * CHUNK + colour * PIECE, PIECE)],
                    gathered.at[part, colour, 0, 0],
                    zr.at[part, colour],
                ).start()

    pl.semaphore_wait(barrier, 34)

    @pl.when(section > 0)
    def _():
        for part in range(per_micro):
            index = section * per_micro + part
            for colour in range(COLOURS):
                pltpu.make_async_remote_copy(
                    src_ref=enter_ref.at[pl.ds(part * CHUNK + colour * PIECE, PIECE)],
                    dst_ref=gathered.at[index, colour, 0, 0],
                    send_sem=fs.at[part, colour],
                    recv_sem=zr.at[index, colour],
                    device_id=mesh_id(0, mp),
                    device_id_type=MESH,
                ).start()

    def swap_weight(rel):
        rows = pl.ds(pl.multiple_of((chip_of(rel) * 2 + 1 - core) * WIDTH, WIDTH), WIDTH)
        return pltpu.make_async_remote_copy(
            src_ref=weight_ref.at[rows],
            dst_ref=w_sib.at[pl.ds(rel * WIDTH, WIDTH)],
            send_sem=once.at[2],
            recv_sem=once.at[3],
            device_id=mesh_id(section, other),
            device_id_type=MESH,
        )

    def columns(rank):
        return pl.ds(pl.multiple_of(rank * WIDTH, WIDTH), WIDTH)

    def spread(source, table, send, receive):
        for other_core in (0, 1):
            for mask_x, mask_y in FAR + (((0, 0),) if other_core else ()):
                rank = (flipped(y, mask_y) * RING + flipped(x, mask_x)) * 2 + (1 - core if other_core else core)
                pltpu.make_async_remote_copy(
                    src_ref=source.at[:, columns(rank)],
                    dst_ref=table.at[mp],
                    send_sem=once.at[send],
                    recv_sem=once.at[receive],
                    device_id=mesh_id(section, rank),
                    device_id_type=MESH,
                ).start()

    def spread_own(source, table, receive):
        pltpu.make_async_copy(source.at[:, columns(mp)], table.at[mp], once.at[receive]).start()

    def full_wait(table, semaphore):
        pltpu.make_async_copy(table, table, once.at[semaphore]).wait()

    def part_wait(table, semaphore):
        part = table.at[pl.ds(0, 31)]
        pltpu.make_async_copy(part, part, once.at[semaphore]).wait()

    for rel in range(16):
        swap_weight(rel).start()
    spread(narrow_ref, narrow_t, 6, 7)
    spread_own(narrow_ref, narrow_t, 7)
    spread(widen_ref, widen_t, 4, 5)
    spread_own(widen_ref, widen_t, 5)
    gain_o[...] = gain_ref[...].astype(jnp.float32)
    for mask_x, mask_y in FAR:
        pltpu.make_async_remote_copy(
            src_ref=gain_o,
            dst_ref=gains.at[mask_y * RING + mask_x],
            send_sem=once.at[8],
            recv_sem=once.at[9],
            device_id=mesh_id(section, (flipped(y, mask_y) * RING + flipped(x, mask_x)) * 2 + core),
            device_id_type=MESH,
        ).start()
    pltpu.make_async_copy(gain_o, gains.at[0], once.at[9]).start()

    def fold_gains():
        full_wait(w_own, 1)
        full_wait(w_sib, 3)
        full_wait(w_sib, 2)
        full_wait(gains, 9)
        pltpu.make_async_copy(gains.at[pl.ds(0, 15)], gains.at[pl.ds(0, 15)], once.at[8]).wait()

        @pl.loop(0, 16)
        def _(rel):
            rows = pl.ds(pl.multiple_of(rel * WIDTH, WIDTH), WIDTH)
            diagonal = lax.broadcasted_iota(jnp.int32, (WIDTH, WIDTH), 0) == lax.broadcasted_iota(
                jnp.int32, (WIDTH, WIDTH), 1
            )
            factor = jnp.sum(jnp.where(diagonal, gains[rel], 0.0), axis=1, keepdims=True)
            w_own[rows] = (w_own[rows].astype(jnp.float32) * factor).astype(jnp.bfloat16)
            w_sib[rows] = (w_sib[rows].astype(jnp.float32) * factor).astype(jnp.bfloat16)

    fold_gains()

    def adapter_of(index):
        return adapter_ref[lax.div(lax.rem(index, per_micro), BLOCK // CHUNK), lax.div(index, per_micro)]

    def partner_of(colour, phase, mask):
        mask_x, mask_y = (mask, 0) if colour == phase else (0, mask)
        return (flipped(y, mask_y) * RING + flipped(x, mask_x)) * 2 + core

    def colour_rows(colour):
        return pl.ds(colour * (PIECE // 2), PIECE // 2)

    def remote(source, target, send, receive, plane, rank):
        return pltpu.make_async_remote_copy(
            src_ref=source,
            dst_ref=target,
            send_sem=send,
            recv_sem=receive,
            device_id=mesh_id(plane, rank),
            device_id_type=MESH,
        )

    def first_rows(index):
        ring_slot = lax.rem(index, DEPTH)
        return [
            remote(
                gathered.at[index, colour, 0, 0],
                gathered.at[index, colour, 0, mask],
                gs.at[ring_slot, 0, colour, mask - 1],
                gr.at[ring_slot, 0, colour, mask - 1],
                section,
                partner_of(colour, 0, mask),
            )
            for mask in (2, 3, 1)
            for colour in range(COLOURS)
        ]

    def first_sums(index):
        ring_slot = lax.rem(index, DEPTH)
        return [
            remote(
                sums_in.at[index, 0, 0, colour_rows(colour)],
                sums_in.at[index, 0, mask, colour_rows(colour)],
                as_.at[ring_slot, 0, colour, mask - 1],
                ar_.at[ring_slot, 0, colour, mask - 1],
                section,
                partner_of(colour, 0, mask),
            )
            for mask in (2, 3, 1)
            for colour in range(COLOURS)
        ]

    def second_copies(index):
        ring_slot = lax.rem(index, DEPTH)
        copies = []
        for mask in (2, 3, 1):
            for colour in range(COLOURS):
                rank = partner_of(colour, 1, mask)
                rows = colour_rows(colour)
                copies.append(
                    remote(
                        gathered.at[index, colour, 0],
                        gathered.at[index, colour, mask],
                        gs.at[ring_slot, 1, colour, mask - 1],
                        gr.at[ring_slot, 1, colour, mask - 1],
                        section,
                        rank,
                    )
                )
                copies.append(
                    remote(
                        sums_out.at[index, rows],
                        sums_in.at[index, 1, mask, rows],
                        as_.at[ring_slot, 1, colour, mask - 1],
                        ar_.at[ring_slot, 1, colour, mask - 1],
                        section,
                        rank,
                    )
                )
        return copies

    def relay(index):
        for copy in first_rows(index) + first_sums(index):
            copy.wait_recv()
        total = sums_in[index, 0, 0].astype(jnp.float32)
        for mask in (1, 2, 3):
            total = total + sums_in[index, 0, mask].astype(jnp.float32)
        running[index] = total
        sums_out[index] = total.astype(jnp.bfloat16)
        for copy in second_copies(index):
            copy.start()

    def finish_gather(index):
        for copy in second_copies(index):
            copy.wait_recv()
        total = running[index]
        for mask in (1, 2, 3):
            total = total + sums_in[index, 1, mask].astype(jnp.float32)
        rows = left_side(index).astype(jnp.float32)
        squares = jnp.sum(rows * rows, axis=1, keepdims=True)
        final_sums[index] = jnp.concatenate(
            [unpack(total), jnp.broadcast_to(squares, (CHUNK, LANES - RANK))], axis=1
        )

    def inner_products(h, scale_by, maps):
        scaled = (h.astype(jnp.float32) * scale_by).astype(jnp.bfloat16)
        inner = lax.dot_general(scaled, maps, (((1,), (1,)), ((), ())), preferred_element_type=jnp.float32)
        return pack(inner).astype(jnp.bfloat16)

    def own_rows(index):
        return jnp.concatenate([gathered[index, colour, 0, 0] for colour in range(COLOURS)], axis=0)

    def feed(index):
        for colour in range(COLOURS):
            piece = gathered.at[index, colour, 0, 0]
            pltpu.make_async_copy(piece, piece, zr.at[index, colour]).wait()
        for copy in first_rows(index):
            copy.start()
        sums_in[index, 0, 0] = inner_products(own_rows(index), gain_o[...], narrow_t[adapter_of(index)])
        for copy in first_sums(index):
            copy.start()

    def left_side(index):
        return jnp.concatenate(
            [
                jnp.concatenate([gathered[(index, colour) + slot_of(colour, rel)] for colour in range(COLOURS)], axis=0)
                for rel in range(16)
            ],
            axis=1,
        )

    def swaps(index):
        ring_slot = lax.rem(index, DEPTH)
        sums = pltpu.make_async_remote_copy(
            src_ref=final_sums.at[index],
            dst_ref=sib_sums.at[index],
            send_sem=xs.at[ring_slot, 0],
            recv_sem=xr.at[ring_slot, 0],
            device_id=mesh_id(section, other),
            device_id_type=MESH,
        )
        parts = pltpu.make_async_remote_copy(
            src_ref=part_out.at[index],
            dst_ref=part_in.at[index],
            send_sem=xs.at[ring_slot, 1],
            recv_sem=xr.at[ring_slot, 1],
            device_id=mesh_id(section, other),
            device_id_type=MESH,
        )
        return sums, parts

    def multiply_sibling(index):
        sums, parts = swaps(index)
        sums.start()
        part_out[index] = jnp.dot(left_side(index), w_sib[...], preferred_element_type=jnp.float32)
        parts.start()

    def multiply_own(index):
        own_part[...] = jnp.dot(left_side(index), w_own[...], preferred_element_type=jnp.float32)

    def onward(index):
        ring_slot = lax.rem(index, DEPTH)
        return [
            remote(
                next_h.at[index, pl.ds(colour * PIECE, PIECE)],
                gathered.at[index, colour, 0, 0],
                zo.at[ring_slot, colour],
                zr.at[index, colour],
                section + 1,
                mp,
            )
            for colour in range(COLOURS)
        ]

    def homeward(index):
        home = lax.div(index, per_micro)
        part = lax.rem(index, per_micro)
        return pltpu.make_async_remote_copy(
            src_ref=next_h.at[index],
            dst_ref=finished.at[part],
            send_sem=zs.at[index],
            recv_sem=fr.at[part],
            device_id=mesh_id(home, mp),
            device_id_type=MESH,
        )

    def combine(index):
        sums, parts = swaps(index)
        sums.wait_recv()
        total = final_sums[index] + sib_sums[index]
        squares = total[:, RANK : RANK + 1]
        scale = lax.rsqrt(squares / (WIDTH * 32) + 1e-05)
        inner = total[:, :RANK].astype(jnp.bfloat16)
        delta = jnp.dot(inner, widen_t[adapter_of(index)], preferred_element_type=jnp.float32)
        own = own_part[...] + 2.0 * delta
        parts.wait_recv()
        base = own + part_in[index]
        h = own_rows(index).astype(jnp.float32)
        result = (h + scale * base).astype(jnp.bfloat16)
        next_h[index] = result

        @pl.when(section < 3)
        def _():
            for copy in onward(index):
                copy.start()

        @pl.when(section == 3)
        def _():
            @pl.when(index < 3 * per_micro)
            def _():
                homeward(index).start()

            @pl.when(index >= 3 * per_micro)
            def _():
                part = lax.rem(index, per_micro)
                pltpu.make_async_copy(next_h.at[index], finished.at[part], fr.at[part]).start()

    def retire(index):
        for copy in first_rows(index) + first_sums(index) + second_copies(index):
            copy.wait_send()
        for copy in swaps(index):
            copy.wait_send()

        @pl.when(section < 3)
        def _():
            for copy in onward(index):
                copy.wait_send()

    full_wait(narrow_t, 7)

    @pl.loop(0, chunks + RETIRE)
    def _(tick):
        @pl.when(tick < chunks)
        def _():
            feed(tick)

        @pl.when(tick == LATE)
        def _():
            part_wait(narrow_t, 6)
            full_wait(widen_t, 5)
            part_wait(widen_t, 4)

        @pl.when((tick >= LATE) & (tick < chunks + LATE))
        def _():
            finish_gather(tick - LATE)
            multiply_sibling(tick - LATE)

        @pl.when((tick >= 1) & (tick <= chunks))
        def _():
            relay(tick - 1)

        @pl.when((tick >= LATE) & (tick < chunks + LATE))
        def _():
            multiply_own(tick - LATE)
            combine(tick - LATE)

        @pl.when(tick >= RETIRE)
        def _():
            retire(tick - RETIRE)

    @pl.when(section > 0)
    def _():
        for part in range(per_micro):
            for colour in range(COLOURS):
                piece = gathered.at[0, colour, 0, 0]
                pltpu.make_async_copy(piece, piece, fs.at[part, colour]).wait()

    @pl.when(section == 3)
    def _():
        @pl.loop(0, 3 * per_micro)
        def _(index):
            pltpu.make_async_copy(next_h.at[index], next_h.at[index], zs.at[index]).wait()

    for part in range(per_micro):
        pltpu.make_async_copy(finished.at[part], finished.at[part], fr.at[part]).wait()
    hidden = jnp.concatenate([finished[part] for part in range(per_micro)], axis=0)
    out_ref[...] = hidden
    head = jnp.broadcast_to(head_ref[...], (8, WIDTH))
    partial = lax.dot_general(head, hidden, (((1,), (1,)), ((), ())), preferred_element_type=jnp.float32)
    score_part[...] = partial[:1]

    def score_send(offset):
        return pltpu.make_async_remote_copy(
            src_ref=score_part,
            dst_ref=score_all.at[mp],
            send_sem=once.at[14],
            recv_sem=once.at[15],
            device_id=mesh_id(section, lax.rem(mp + offset, 32)),
            device_id_type=MESH,
        )

    @pl.loop(1, 32)
    def _(offset):
        score_send(offset).start()

    pltpu.make_async_copy(score_part, score_all.at[mp], once.at[15]).start()
    pltpu.make_async_copy(score_all, score_all, once.at[15]).wait()
    pltpu.make_async_copy(score_all.at[pl.ds(0, 31)], score_all.at[pl.ds(0, 31)], once.at[14]).wait()
    raw = jnp.sum(score_all[...], axis=0)
    place = lax.broadcasted_iota(jnp.int32, (1, 2 * BLOCK), 1)
    limit = jnp.where(place < BLOCK, live_ref[0, 0], live_ref[0, 1])
    score_ref[...] = jnp.where(lax.rem(place, BLOCK) < limit, raw, 0.0)


def shards(
    entering_hidden,
    section_weight,
    section_norm_gain,
    plugin_narrowing_factors,
    plugin_widening_factors,
    reward_head,
    adapter_of_block,
    live_block_rows,
):
    chunks = 1024 // CHUNK
    bf16, f32 = jnp.bfloat16, jnp.float32
    vmem = pl.BlockSpec(memory_space=pltpu.VMEM)
    smem = pl.BlockSpec(memory_space=pltpu.SMEM)
    anywhere = pl.BlockSpec(memory_space=pl.ANY)
    dma = pltpu.SemaphoreType.DMA
    hidden, scores = pl.pallas_call(
        functools.partial(kernel, chunks),
        out_shape=(
            jax.ShapeDtypeStruct((256, WIDTH), bf16),
            jax.ShapeDtypeStruct((1, 256), f32),
        ),
        in_specs=[smem, smem, anywhere, anywhere, vmem, anywhere, anywhere, vmem],
        out_specs=(vmem, vmem),
        scratch_shapes=[
            pltpu.VMEM((chunks, COLOURS, RING, RING, PIECE, WIDTH), bf16),
            pltpu.VMEM((chunks, CHUNK // 2, LANES), bf16),
            pltpu.VMEM((chunks, PHASES, RING, CHUNK // 2, LANES), bf16),
            pltpu.VMEM((chunks, CHUNK // 2, LANES), f32),
            pltpu.VMEM((chunks, CHUNK, LANES), f32),
            pltpu.VMEM((chunks, CHUNK, LANES), f32),
            pltpu.VMEM((chunks, CHUNK, WIDTH), f32),
            pltpu.VMEM((chunks, CHUNK, WIDTH), f32),
            pltpu.VMEM((CHUNK, WIDTH), f32),
            pltpu.VMEM((chunks, CHUNK, WIDTH), bf16),
            pltpu.VMEM((16 * WIDTH, WIDTH), bf16),
            pltpu.VMEM((16 * WIDTH, WIDTH), bf16),
            pltpu.VMEM((32, RANK, WIDTH), bf16),
            pltpu.VMEM((32, RANK, WIDTH), bf16),
            pltpu.VMEM((1, WIDTH), f32),
            pltpu.VMEM((16, 1, WIDTH), f32),
            pltpu.VMEM((256 // CHUNK, CHUNK, WIDTH), bf16),
            pltpu.VMEM((1, 256), f32),
            pltpu.VMEM((32, 1, 256), f32),
            dma((DEPTH, PHASES, COLOURS, 3)),
            dma((DEPTH, PHASES, COLOURS, 3)),
            dma((DEPTH, PHASES, COLOURS, 3)),
            dma((DEPTH, PHASES, COLOURS, 3)),
            dma((DEPTH, 2)),
            dma((DEPTH, 2)),
            dma((chunks,)),
            dma((DEPTH, COLOURS)),
            dma((chunks, COLOURS)),
            dma((4, COLOURS)),
            dma((4,)),
            dma((16,)),
        ],
        compiler_params=pltpu.CompilerParams(
            collective_id=0, has_side_effects=True, vmem_limit_bytes=60 * 1024 * 1024
        ),
    )(
        adapter_of_block.T,
        live_block_rows,
        entering_hidden[0],
        section_weight[0],
        section_norm_gain,
        plugin_narrowing_factors[0, 0].T,
        plugin_widening_factors[0, 0],
        reward_head[None, :],
    )
    return hidden[None], scores


def solution(mesh):
    placed = (
        P("section", None, "mp"),
        P("section", None, "mp"),
        P("section", "mp"),
        P("section", "mp", None, None),
        P("section", "mp", None, None),
        P("mp"),
        P(),
        P("section", None),
    )
    return jax.shard_map(
        shards,
        mesh=mesh,
        in_specs=placed,
        out_specs=(P("section", None, "mp"), P("section", None)),
        check_vma=False,
    )
```

```python
import functools

import jax
import jax.numpy as jnp
from jax import lax
from jax.experimental import pallas as pl
from jax.experimental.pallas import tpu as pltpu
from jax.sharding import PartitionSpec as P

MESH = pl.DeviceIdType.MESH
BLOCK = 128
CHUNK = 64
COLOURS = 2
PHASES = 2
PIECE = CHUNK // COLOURS
RING = 4
WIDTH = 256
RANK = 64
LANES = 128
LATE = 4
RETIRE = 5
DEPTH = 6

FAR = ((2, 2), (3, 2), (2, 3), (1, 2), (2, 1), (0, 2), (2, 0), (3, 1), (1, 3), (3, 3), (1, 1), (0, 3), (3, 0), (0, 1), (1, 0))


def flipped(position, mask):
    if mask == 0:
        return position
    if mask == 1:
        return position + 1 - 2 * lax.rem(position, 2)
    if mask == 2:
        return lax.rem(position + 2, 4)
    return 3 - position


def slot_of(colour, rel):
    return (rel // 4, rel % 4) if colour == 0 else (rel % 4, rel // 4)


def pack(value):
    pieces = []
    for colour in range(COLOURS):
        first = colour * PIECE
        pieces.append(
            jnp.concatenate([value[first : first + PIECE // 2], value[first + PIECE // 2 : first + PIECE]], axis=1)
        )
    return jnp.concatenate(pieces, axis=0)


def unpack(value):
    pieces = []
    for colour in range(COLOURS):
        piece = value[colour * PIECE // 2 : (colour + 1) * PIECE // 2]
        pieces += [piece[:, :RANK], piece[:, RANK:]]
    return jnp.concatenate(pieces, axis=0)


def kernel(
    chunks,
    adapter_ref,
    live_ref,
    enter_ref,
    weight_ref,
    gain_ref,
    narrow_ref,
    widen_ref,
    head_ref,
    out_ref,
    score_ref,
    gathered,
    sums_out,
    sums_in,
    running,
    final_sums,
    sib_sums,
    part_out,
    part_in,
    own_part,
    next_h,
    w_own,
    w_sib,
    narrow_s,
    widen_s,
    narrow_t,
    widen_t,
    gain_o,
    gains,
    finished,
    score_part,
    score_all,
    gs,
    gr,
    as_,
    ar_,
    ts,
    tr,
    xs,
    xr,
    zs,
    zo,
    zr,
    fs,
    fr,
    once,
):
    section = lax.axis_index("section")
    mp = lax.axis_index("mp")
    core = lax.rem(mp, 2)
    chip = lax.div(mp, 2)
    x = lax.rem(chip, RING)
    y = lax.div(chip, RING)
    other = mp + 1 - 2 * core
    per_micro = 256 // CHUNK

    def mesh_id(where, rank):
        return {"section": where, "mp": rank}

    barrier = pltpu.get_barrier_semaphore()
    for offset in range(1, 32):
        pl.semaphore_signal(
            barrier, inc=1, device_id=mesh_id(section, lax.rem(mp + offset, 32)), device_id_type=MESH
        )
    for offset in range(1, 4):
        pl.semaphore_signal(
            barrier, inc=1, device_id=mesh_id(lax.rem(section + offset, 4), mp), device_id_type=MESH
        )

    def chip_of(rel):
        return flipped(y, rel // 4) * RING + flipped(x, rel % 4)

    for rel in range(16):
        rows = pl.ds(pl.multiple_of((chip_of(rel) * 2 + core) * WIDTH, WIDTH), WIDTH)
        pltpu.make_async_copy(
            weight_ref.at[rows], w_own.at[pl.ds(rel * WIDTH, WIDTH)], once.at[1]
        ).start()

    def columns(rank):
        return pl.ds(pl.multiple_of(rank * WIDTH, WIDTH), WIDTH)

    for rank in range(32):
        pltpu.make_async_copy(narrow_ref.at[:, columns(rank)], narrow_s.at[rank], once.at[0]).start()
    for rank in range(32):
        pltpu.make_async_copy(widen_ref.at[:, columns(rank)], widen_s.at[rank], once.at[10]).start()

    @pl.when(section == 0)
    def _():
        for part in range(per_micro):
            for colour in range(COLOURS):
                pltpu.make_async_copy(
                    enter_ref.at[pl.ds(part * CHUNK + colour * PIECE, PIECE)],
                    gathered.at[part, colour, 0, 0],
                    zr.at[part, colour],
                ).start()

    pl.semaphore_wait(barrier, 34)

    @pl.when(section > 0)
    def _():
        for part in range(per_micro):
            index = section * per_micro + part
            for colour in range(COLOURS):
                pltpu.make_async_remote_copy(
                    src_ref=enter_ref.at[pl.ds(part * CHUNK + colour * PIECE, PIECE)],
                    dst_ref=gathered.at[index, colour, 0, 0],
                    send_sem=fs.at[part, colour],
                    recv_sem=zr.at[index, colour],
                    device_id=mesh_id(0, mp),
                    device_id_type=MESH,
                ).start()

    def swap_weight(rel):
        rows = pl.ds(pl.multiple_of((chip_of(rel) * 2 + 1 - core) * WIDTH, WIDTH), WIDTH)
        return pltpu.make_async_remote_copy(
            src_ref=weight_ref.at[rows],
            dst_ref=w_sib.at[pl.ds(rel * WIDTH, WIDTH)],
            send_sem=once.at[2],
            recv_sem=once.at[3],
            device_id=mesh_id(section, other),
            device_id_type=MESH,
        )

    def spread(source, table, send, receive):
        for other_core in (0, 1):
            for mask_x, mask_y in FAR + (((0, 0),) if other_core else ()):
                rank = (flipped(y, mask_y) * RING + flipped(x, mask_x)) * 2 + (1 - core if other_core else core)
                pltpu.make_async_remote_copy(
                    src_ref=source.at[rank],
                    dst_ref=table.at[mp],
                    send_sem=once.at[send],
                    recv_sem=once.at[receive],
                    device_id=mesh_id(section, rank),
                    device_id_type=MESH,
                ).start()

    def spread_own(source, table, receive):
        pltpu.make_async_copy(source.at[mp], table.at[mp], once.at[receive]).start()

    def full_wait(table, semaphore):
        pltpu.make_async_copy(table, table, once.at[semaphore]).wait()

    def part_wait(table, semaphore):
        part = table.at[pl.ds(0, 31)]
        pltpu.make_async_copy(part, part, once.at[semaphore]).wait()

    full_wait(narrow_s, 0)
    spread(narrow_s, narrow_t, 6, 7)
    spread_own(narrow_s, narrow_t, 7)
    full_wait(widen_s, 10)
    spread(widen_s, widen_t, 4, 5)
    spread_own(widen_s, widen_t, 5)
    for rel in range(16):
        swap_weight(rel).start()
    gain_o[...] = gain_ref[...].astype(jnp.float32)
    for mask_x, mask_y in FAR:
        pltpu.make_async_remote_copy(
            src_ref=gain_o,
            dst_ref=gains.at[mask_y * RING + mask_x],
            send_sem=once.at[8],
            recv_sem=once.at[9],
            device_id=mesh_id(section, (flipped(y, mask_y) * RING + flipped(x, mask_x)) * 2 + core),
            device_id_type=MESH,
        ).start()
    pltpu.make_async_copy(gain_o, gains.at[0], once.at[9]).start()

    def fold_gains():
        full_wait(w_own, 1)
        full_wait(w_sib, 3)
        full_wait(w_sib, 2)
        full_wait(gains, 9)
        pltpu.make_async_copy(gains.at[pl.ds(0, 15)], gains.at[pl.ds(0, 15)], once.at[8]).wait()

        @pl.loop(0, 16)
        def _(rel):
            rows = pl.ds(pl.multiple_of(rel * WIDTH, WIDTH), WIDTH)
            diagonal = lax.broadcasted_iota(jnp.int32, (WIDTH, WIDTH), 0) == lax.broadcasted_iota(
                jnp.int32, (WIDTH, WIDTH), 1
            )
            factor = jnp.sum(jnp.where(diagonal, gains[rel], 0.0), axis=1, keepdims=True)
            w_own[rows] = (w_own[rows].astype(jnp.float32) * factor).astype(jnp.bfloat16)
            w_sib[rows] = (w_sib[rows].astype(jnp.float32) * factor).astype(jnp.bfloat16)

    fold_gains()

    def adapter_of(index):
        return adapter_ref[lax.div(lax.rem(index, per_micro), BLOCK // CHUNK), lax.div(index, per_micro)]

    def partner_of(colour, phase, mask):
        mask_x, mask_y = (mask, 0) if colour == phase else (0, mask)
        return (flipped(y, mask_y) * RING + flipped(x, mask_x)) * 2 + core

    def colour_rows(colour):
        return pl.ds(colour * (PIECE // 2), PIECE // 2)

    def remote(source, target, send, receive, plane, rank):
        return pltpu.make_async_remote_copy(
            src_ref=source,
            dst_ref=target,
            send_sem=send,
            recv_sem=receive,
            device_id=mesh_id(plane, rank),
            device_id_type=MESH,
        )

    def first_rows(index):
        ring_slot = lax.rem(index, DEPTH)
        return [
            remote(
                gathered.at[index, colour, 0, 0],
                gathered.at[index, colour, 0, mask],
                gs.at[ring_slot, 0, colour, mask - 1],
                gr.at[ring_slot, 0, colour, mask - 1],
                section,
                partner_of(colour, 0, mask),
            )
            for mask in (2, 3, 1)
            for colour in range(COLOURS)
        ]

    def first_sums(index):
        ring_slot = lax.rem(index, DEPTH)
        return [
            remote(
                sums_in.at[index, 0, 0, colour_rows(colour)],
                sums_in.at[index, 0, mask, colour_rows(colour)],
                as_.at[ring_slot, 0, colour, mask - 1],
                ar_.at[ring_slot, 0, colour, mask - 1],
                section,
                partner_of(colour, 0, mask),
            )
            for mask in (2, 3, 1)
            for colour in range(COLOURS)
        ]

    def second_rows(index):
        ring_slot = lax.rem(index, DEPTH)
        return [
            remote(
                gathered.at[index, colour, 0],
                gathered.at[index, colour, mask],
                gs.at[ring_slot, 1, colour, mask - 1],
                gr.at[ring_slot, 1, colour, mask - 1],
                section,
                partner_of(colour, 1, mask),
            )
            for mask in (3, 1)
            for colour in range(COLOURS)
        ]

    def third_rows(index):
        ring_slot = lax.rem(index, DEPTH)
        return [
            remote(
                gathered.at[index, colour, 4 - mask, pl.ds(half, 2)],
                gathered.at[index, colour, 2, pl.ds(half, 2)],
                ts.at[ring_slot, colour, half // 2],
                tr.at[ring_slot, colour, half // 2],
                section,
                partner_of(colour, 1, mask),
            )
            for mask, half in ((1, 0), (3, 2))
            for colour in range(COLOURS)
        ]

    def second_sums(index):
        ring_slot = lax.rem(index, DEPTH)
        return [
            remote(
                sums_out.at[index, colour_rows(colour)],
                sums_in.at[index, 1, mask, colour_rows(colour)],
                as_.at[ring_slot, 1, colour, mask - 1],
                ar_.at[ring_slot, 1, colour, mask - 1],
                section,
                partner_of(colour, 1, mask),
            )
            for mask in (2, 3, 1)
            for colour in range(COLOURS)
        ]

    def forward(index):
        for copy in second_rows(index):
            copy.wait_recv()
        for copy in third_rows(index):
            copy.start()

    def relay(index):
        for copy in first_rows(index):
            copy.wait_recv()
        for copy in second_rows(index):
            copy.start()
        for copy in first_sums(index):
            copy.wait_recv()
        total = sums_in[index, 0, 0].astype(jnp.float32)
        for mask in (1, 2, 3):
            total = total + sums_in[index, 0, mask].astype(jnp.float32)
        running[index] = total
        sums_out[index] = total.astype(jnp.bfloat16)
        for copy in second_sums(index):
            copy.start()

    def finish_gather(index):
        for copy in second_sums(index) + third_rows(index):
            copy.wait_recv()
        total = running[index]
        for mask in (1, 2, 3):
            total = total + sums_in[index, 1, mask].astype(jnp.float32)
        rows = left_side(index).astype(jnp.float32)
        squares = jnp.sum(rows * rows, axis=1, keepdims=True)
        final_sums[index] = jnp.concatenate(
            [unpack(total), jnp.broadcast_to(squares, (CHUNK, LANES - RANK))], axis=1
        )

    def inner_products(h, scale_by, maps):
        scaled = (h.astype(jnp.float32) * scale_by).astype(jnp.bfloat16)
        inner = lax.dot_general(scaled, maps, (((1,), (1,)), ((), ())), preferred_element_type=jnp.float32)
        return pack(inner).astype(jnp.bfloat16)

    def own_rows(index):
        return jnp.concatenate([gathered[index, colour, 0, 0] for colour in range(COLOURS)], axis=0)

    def feed(index):
        for colour in range(COLOURS):
            piece = gathered.at[index, colour, 0, 0]
            pltpu.make_async_copy(piece, piece, zr.at[index, colour]).wait()
        for copy in first_rows(index):
            copy.start()
        sums_in[index, 0, 0] = inner_products(own_rows(index), gain_o[...], narrow_t[adapter_of(index)])
        for copy in first_sums(index):
            copy.start()

    def left_side(index):
        return jnp.concatenate(
            [
                jnp.concatenate([gathered[(index, colour) + slot_of(colour, rel)] for colour in range(COLOURS)], axis=0)
                for rel in range(16)
            ],
            axis=1,
        )

    def swaps(index):
        ring_slot = lax.rem(index, DEPTH)
        sums = pltpu.make_async_remote_copy(
            src_ref=final_sums.at[index],
            dst_ref=sib_sums.at[index],
            send_sem=xs.at[ring_slot, 0],
            recv_sem=xr.at[ring_slot, 0],
            device_id=mesh_id(section, other),
            device_id_type=MESH,
        )
        parts = pltpu.make_async_remote_copy(
            src_ref=part_out.at[index],
            dst_ref=part_in.at[index],
            send_sem=xs.at[ring_slot, 1],
            recv_sem=xr.at[ring_slot, 1],
            device_id=mesh_id(section, other),
            device_id_type=MESH,
        )
        return sums, parts

    def multiply_sibling(index):
        sums, parts = swaps(index)
        sums.start()
        part_out[index] = jnp.dot(left_side(index), w_sib[...], preferred_element_type=jnp.float32)
        parts.start()

    def multiply_own(index):
        own_part[...] = jnp.dot(left_side(index), w_own[...], preferred_element_type=jnp.float32)

    def onward(index):
        ring_slot = lax.rem(index, DEPTH)
        return [
            remote(
                next_h.at[index, pl.ds(colour * PIECE, PIECE)],
                gathered.at[index, colour, 0, 0],
                zo.at[ring_slot, colour],
                zr.at[index, colour],
                section + 1,
                mp,
            )
            for colour in range(COLOURS)
        ]

    def homeward(index):
        home = lax.div(index, per_micro)
        part = lax.rem(index, per_micro)
        return pltpu.make_async_remote_copy(
            src_ref=next_h.at[index],
            dst_ref=finished.at[part],
            send_sem=zs.at[index],
            recv_sem=fr.at[part],
            device_id=mesh_id(home, mp),
            device_id_type=MESH,
        )

    def combine(index):
        sums, parts = swaps(index)
        sums.wait_recv()
        total = final_sums[index] + sib_sums[index]
        squares = total[:, RANK : RANK + 1]
        scale = lax.rsqrt(squares / (WIDTH * 32) + 1e-05)
        inner = total[:, :RANK].astype(jnp.bfloat16)
        delta = jnp.dot(inner, widen_t[adapter_of(index)], preferred_element_type=jnp.float32)
        own = own_part[...] + 2.0 * delta
        parts.wait_recv()
        base = own + part_in[index]
        h = own_rows(index).astype(jnp.float32)
        result = (h + scale * base).astype(jnp.bfloat16)
        next_h[index] = result

        @pl.when(section < 3)
        def _():
            for copy in onward(index):
                copy.start()

        @pl.when(section == 3)
        def _():
            @pl.when(index < 3 * per_micro)
            def _():
                homeward(index).start()

            @pl.when(index >= 3 * per_micro)
            def _():
                part = lax.rem(index, per_micro)
                pltpu.make_async_copy(next_h.at[index], finished.at[part], fr.at[part]).start()

    def retire(index):
        for copy in first_rows(index) + first_sums(index) + second_rows(index) + second_sums(index) + third_rows(index):
            copy.wait_send()
        for copy in swaps(index):
            copy.wait_send()

        @pl.when(section < 3)
        def _():
            for copy in onward(index):
                copy.wait_send()

    full_wait(narrow_t, 7)

    @pl.loop(0, chunks + RETIRE)
    def _(tick):
        @pl.when(tick < chunks)
        def _():
            feed(tick)

        @pl.when(tick == LATE)
        def _():
            part_wait(narrow_t, 6)
            full_wait(widen_t, 5)
            part_wait(widen_t, 4)

        @pl.when((tick >= LATE) & (tick < chunks + LATE))
        def _():
            finish_gather(tick - LATE)
            multiply_sibling(tick - LATE)

        @pl.when((tick >= 1) & (tick <= chunks))
        def _():
            relay(tick - 1)

        @pl.when((tick >= LATE) & (tick < chunks + LATE))
        def _():
            multiply_own(tick - LATE)
            combine(tick - LATE)

        @pl.when((tick >= 2) & (tick <= chunks + 1))
        def _():
            forward(tick - 2)

        @pl.when(tick >= RETIRE)
        def _():
            retire(tick - RETIRE)

    @pl.when(section > 0)
    def _():
        for part in range(per_micro):
            for colour in range(COLOURS):
                piece = gathered.at[0, colour, 0, 0]
                pltpu.make_async_copy(piece, piece, fs.at[part, colour]).wait()

    @pl.when(section == 3)
    def _():
        @pl.loop(0, 3 * per_micro)
        def _(index):
            pltpu.make_async_copy(next_h.at[index], next_h.at[index], zs.at[index]).wait()

    for part in range(per_micro):
        pltpu.make_async_copy(finished.at[part], finished.at[part], fr.at[part]).wait()
    hidden = jnp.concatenate([finished[part] for part in range(per_micro)], axis=0)
    out_ref[...] = hidden
    head = jnp.broadcast_to(head_ref[...].reshape(1, WIDTH), (8, WIDTH))
    partial = lax.dot_general(head, hidden, (((1,), (1,)), ((), ())), preferred_element_type=jnp.float32)
    score_part[...] = partial[:1]

    def score_send(offset):
        return pltpu.make_async_remote_copy(
            src_ref=score_part,
            dst_ref=score_all.at[mp],
            send_sem=once.at[14],
            recv_sem=once.at[15],
            device_id=mesh_id(section, lax.rem(mp + offset, 32)),
            device_id_type=MESH,
        )

    @pl.loop(1, 32)
    def _(offset):
        score_send(offset).start()

    pltpu.make_async_copy(score_part, score_all.at[mp], once.at[15]).start()
    pltpu.make_async_copy(score_all, score_all, once.at[15]).wait()
    pltpu.make_async_copy(score_all.at[pl.ds(0, 31)], score_all.at[pl.ds(0, 31)], once.at[14]).wait()
    raw = jnp.sum(score_all[...], axis=0)
    place = lax.broadcasted_iota(jnp.int32, (1, 2 * BLOCK), 1)
    limit = jnp.where(place < BLOCK, live_ref[0, 0], live_ref[0, 1])
    score_ref[...] = jnp.where(lax.rem(place, BLOCK) < limit, raw, 0.0)


def shards(
    entering_hidden,
    section_weight,
    section_norm_gain,
    plugin_narrowing_factors,
    plugin_widening_factors,
    reward_head,
    adapter_of_block,
    live_block_rows,
):
    chunks = 1024 // CHUNK
    bf16, f32 = jnp.bfloat16, jnp.float32
    vmem = pl.BlockSpec(memory_space=pltpu.VMEM)
    smem = pl.BlockSpec(memory_space=pltpu.SMEM)
    anywhere = pl.BlockSpec(memory_space=pl.ANY)
    dma = pltpu.SemaphoreType.DMA
    hidden, scores = pl.pallas_call(
        functools.partial(kernel, chunks),
        out_shape=(
            jax.ShapeDtypeStruct((256, WIDTH), bf16),
            jax.ShapeDtypeStruct((1, 256), f32),
        ),
        in_specs=[smem, smem, anywhere, anywhere, vmem, anywhere, anywhere, vmem],
        out_specs=(vmem, vmem),
        scratch_shapes=[
            pltpu.VMEM((chunks, COLOURS, RING, RING, PIECE, WIDTH), bf16),
            pltpu.VMEM((chunks, CHUNK // 2, LANES), bf16),
            pltpu.VMEM((chunks, PHASES, RING, CHUNK // 2, LANES), bf16),
            pltpu.VMEM((chunks, CHUNK // 2, LANES), f32),
            pltpu.VMEM((chunks, CHUNK, LANES), f32),
            pltpu.VMEM((chunks, CHUNK, LANES), f32),
            pltpu.VMEM((chunks, CHUNK, WIDTH), f32),
            pltpu.VMEM((chunks, CHUNK, WIDTH), f32),
            pltpu.VMEM((CHUNK, WIDTH), f32),
            pltpu.VMEM((chunks, CHUNK, WIDTH), bf16),
            pltpu.VMEM((16 * WIDTH, WIDTH), bf16),
            pltpu.VMEM((16 * WIDTH, WIDTH), bf16),
            pltpu.VMEM((32, RANK, WIDTH), bf16),
            pltpu.VMEM((32, RANK, WIDTH), bf16),
            pltpu.VMEM((32, RANK, WIDTH), bf16),
            pltpu.VMEM((32, RANK, WIDTH), bf16),
            pltpu.VMEM((1, WIDTH), f32),
            pltpu.VMEM((16, 1, WIDTH), f32),
            pltpu.VMEM((256 // CHUNK, CHUNK, WIDTH), bf16),
            pltpu.VMEM((1, 256), f32),
            pltpu.VMEM((32, 1, 256), f32),
            dma((DEPTH, PHASES, COLOURS, 3)),
            dma((DEPTH, PHASES, COLOURS, 3)),
            dma((DEPTH, PHASES, COLOURS, 3)),
            dma((DEPTH, PHASES, COLOURS, 3)),
            dma((DEPTH, COLOURS, 2)),
            dma((DEPTH, COLOURS, 2)),
            dma((DEPTH, 2)),
            dma((DEPTH, 2)),
            dma((chunks,)),
            dma((DEPTH, COLOURS)),
            dma((chunks, COLOURS)),
            dma((4, COLOURS)),
            dma((4,)),
            dma((16,)),
        ],
        compiler_params=pltpu.CompilerParams(
            collective_id=0, has_side_effects=True, vmem_limit_bytes=60 * 1024 * 1024
        ),
    )(
        adapter_of_block.T,
        live_block_rows,
        entering_hidden[0],
        section_weight[0],
        section_norm_gain,
        plugin_narrowing_factors[0, 0].T,
        plugin_widening_factors[0, 0],
        reward_head,
    )
    return hidden[None], scores


def solution(mesh):
    placed = (
        P("section", None, "mp"),
        P("section", None, "mp"),
        P("section", "mp"),
        P("section", "mp", None, None),
        P("section", "mp", None, None),
        P("mp"),
        P(),
        P("section", None),
    )
    return jax.shard_map(
        shards,
        mesh=mesh,
        in_specs=placed,
        out_specs=(P("section", None, "mp"), P("section", None)),
        check_vma=False,
    )
```

```python
import functools

import jax
import jax.numpy as jnp
from jax import lax
from jax.experimental import pallas as pl
from jax.experimental.pallas import tpu as pltpu
from jax.sharding import PartitionSpec as P

MESH = pl.DeviceIdType.MESH
BLOCK = 128
CHUNK = 64
COLOURS = 2
PHASES = 2
PIECE = CHUNK // COLOURS
RING = 4
WIDTH = 256
RANK = 64
LANES = 128
LATE = 4
RETIRE = 5
DEPTH = 6

FAR = ((2, 2), (3, 2), (2, 3), (1, 2), (2, 1), (0, 2), (2, 0), (3, 1), (1, 3), (3, 3), (1, 1), (0, 3), (3, 0), (0, 1), (1, 0))


def flipped(position, mask):
    if mask == 0:
        return position
    if mask == 1:
        return position + 1 - 2 * lax.rem(position, 2)
    if mask == 2:
        return lax.rem(position + 2, 4)
    return 3 - position


def slot_of(colour, rel):
    return (rel // 4, rel % 4) if colour == 0 else (rel % 4, rel // 4)


def pack(value):
    pieces = []
    for colour in range(COLOURS):
        first = colour * PIECE
        pieces.append(
            jnp.concatenate([value[first : first + PIECE // 2], value[first + PIECE // 2 : first + PIECE]], axis=1)
        )
    return jnp.concatenate(pieces, axis=0)


def unpack(value):
    pieces = []
    for colour in range(COLOURS):
        piece = value[colour * PIECE // 2 : (colour + 1) * PIECE // 2]
        pieces += [piece[:, :RANK], piece[:, RANK:]]
    return jnp.concatenate(pieces, axis=0)


def kernel(
    chunks,
    adapter_ref,
    live_ref,
    enter_ref,
    weight_ref,
    gain_ref,
    narrow_ref,
    widen_ref,
    head_ref,
    out_ref,
    score_ref,
    gathered,
    sums_out,
    sums_in,
    running,
    final_sums,
    sib_sums,
    part_out,
    part_in,
    own_part,
    next_h,
    w_own,
    w_sib,
    narrow_s,
    widen_s,
    relay_s,
    narrow_t,
    widen_t,
    gain_o,
    gains,
    finished,
    score_part,
    score_all,
    gs,
    gr,
    as_,
    ar_,
    ts,
    tr,
    xs,
    xr,
    zs,
    zo,
    zr,
    fs,
    fr,
    once,
):
    section = lax.axis_index("section")
    mp = lax.axis_index("mp")
    core = lax.rem(mp, 2)
    chip = lax.div(mp, 2)
    x = lax.rem(chip, RING)
    y = lax.div(chip, RING)
    other = mp + 1 - 2 * core
    per_micro = 256 // CHUNK

    def mesh_id(where, rank):
        return {"section": where, "mp": rank}

    barrier = pltpu.get_barrier_semaphore()
    for offset in range(1, 32):
        pl.semaphore_signal(
            barrier, inc=1, device_id=mesh_id(section, lax.rem(mp + offset, 32)), device_id_type=MESH
        )
    for offset in range(1, 4):
        pl.semaphore_signal(
            barrier, inc=1, device_id=mesh_id(lax.rem(section + offset, 4), mp), device_id_type=MESH
        )

    def chip_of(rel):
        return flipped(y, rel // 4) * RING + flipped(x, rel % 4)

    for rel in range(16):
        rows = pl.ds(pl.multiple_of((chip_of(rel) * 2 + core) * WIDTH, WIDTH), WIDTH)
        pltpu.make_async_copy(
            weight_ref.at[rows], w_own.at[pl.ds(rel * WIDTH, WIDTH)], once.at[1]
        ).start()

    def columns(rank):
        return pl.ds(pl.multiple_of(rank * WIDTH, WIDTH), WIDTH)

    def stage(rank):
        return lax.rem(rank, 2) * 16 + lax.div(rank, 2)

    for rank in range(32):
        slot = rank % 2 * 16 + rank // 2
        pltpu.make_async_copy(narrow_ref.at[:, columns(rank)], narrow_s.at[slot], once.at[0]).start()
        pltpu.make_async_copy(widen_ref.at[:, columns(rank)], widen_s.at[slot], once.at[10]).start()

    @pl.when(section == 0)
    def _():
        for part in range(per_micro):
            for colour in range(COLOURS):
                pltpu.make_async_copy(
                    enter_ref.at[pl.ds(part * CHUNK + colour * PIECE, PIECE)],
                    gathered.at[part, colour, 0, 0],
                    zr.at[part, colour],
                ).start()

    pl.semaphore_wait(barrier, 34)

    @pl.when(section > 0)
    def _():
        for part in range(per_micro):
            index = section * per_micro + part
            for colour in range(COLOURS):
                pltpu.make_async_remote_copy(
                    src_ref=enter_ref.at[pl.ds(part * CHUNK + colour * PIECE, PIECE)],
                    dst_ref=gathered.at[index, colour, 0, 0],
                    send_sem=fs.at[part, colour],
                    recv_sem=zr.at[index, colour],
                    device_id=mesh_id(0, mp),
                    device_id_type=MESH,
                ).start()

    def swap_weight(rel):
        rows = pl.ds(pl.multiple_of((chip_of(rel) * 2 + 1 - core) * WIDTH, WIDTH), WIDTH)
        return pltpu.make_async_remote_copy(
            src_ref=weight_ref.at[rows],
            dst_ref=w_sib.at[pl.ds(rel * WIDTH, WIDTH)],
            send_sem=once.at[2],
            recv_sem=once.at[3],
            device_id=mesh_id(section, other),
            device_id_type=MESH,
        )

    def spread(source, table, send, receive):
        for other_core in (0, 1):
            for mask_x, mask_y in FAR + (((0, 0),) if other_core else ()):
                rank = (flipped(y, mask_y) * RING + flipped(x, mask_x)) * 2 + (1 - core if other_core else core)
                pltpu.make_async_remote_copy(
                    src_ref=source.at[stage(rank)],
                    dst_ref=table.at[mp],
                    send_sem=once.at[send],
                    recv_sem=once.at[receive],
                    device_id=mesh_id(section, rank),
                    device_id_type=MESH,
                ).start()

    def spread_own(source, table, receive):
        pltpu.make_async_copy(source.at[stage(mp)], table.at[mp], once.at[receive]).start()

    def full_wait(table, semaphore):
        pltpu.make_async_copy(table, table, once.at[semaphore]).wait()

    def part_wait(table, semaphore):
        part = table.at[pl.ds(0, 31)]
        pltpu.make_async_copy(part, part, once.at[semaphore]).wait()

    full_wait(widen_s, 10)

    def aside(half):
        return pltpu.make_async_remote_copy(
            src_ref=widen_s.at[pl.ds(half * 16, 16)],
            dst_ref=relay_s,
            send_sem=once.at[16 + half],
            recv_sem=once.at[18],
            device_id=mesh_id(2 * half + 1, mp),
            device_id_type=MESH,
        )

    @pl.when(section == 0)
    def _():
        for half in (0, 1):
            aside(half).start()

    full_wait(narrow_s, 0)
    spread(narrow_s, narrow_t, 6, 7)
    spread_own(narrow_s, narrow_t, 7)

    for rel in range(16):
        swap_weight(rel).start()
    gain_o[...] = gain_ref[...].astype(jnp.float32)
    for mask_x, mask_y in FAR:
        pltpu.make_async_remote_copy(
            src_ref=gain_o,
            dst_ref=gains.at[mask_y * RING + mask_x],
            send_sem=once.at[8],
            recv_sem=once.at[9],
            device_id=mesh_id(section, (flipped(y, mask_y) * RING + flipped(x, mask_x)) * 2 + core),
            device_id_type=MESH,
        ).start()
    pltpu.make_async_copy(gain_o, gains.at[0], once.at[9]).start()

    def fold_gains():
        full_wait(w_own, 1)
        full_wait(w_sib, 3)
        full_wait(w_sib, 2)
        full_wait(gains, 9)
        pltpu.make_async_copy(gains.at[pl.ds(0, 15)], gains.at[pl.ds(0, 15)], once.at[8]).wait()

        @pl.loop(0, 16)
        def _(rel):
            rows = pl.ds(pl.multiple_of(rel * WIDTH, WIDTH), WIDTH)
            diagonal = lax.broadcasted_iota(jnp.int32, (WIDTH, WIDTH), 0) == lax.broadcasted_iota(
                jnp.int32, (WIDTH, WIDTH), 1
            )
            factor = jnp.sum(jnp.where(diagonal, gains[rel], 0.0), axis=1, keepdims=True)
            w_own[rows] = (w_own[rows].astype(jnp.float32) * factor).astype(jnp.bfloat16)
            w_sib[rows] = (w_sib[rows].astype(jnp.float32) * factor).astype(jnp.bfloat16)

    fold_gains()

    @pl.when(lax.rem(section, 2) == 1)
    def _():
        full_wait(relay_s, 18)
        for mask_x, mask_y in FAR + ((0, 0),):
            target = flipped(y, mask_y) * RING + flipped(x, mask_x)
            pltpu.make_async_remote_copy(
                src_ref=relay_s.at[target],
                dst_ref=widen_t.at[mp],
                send_sem=once.at[19],
                recv_sem=once.at[5],
                device_id=mesh_id(0, target * 2 + lax.div(section, 2)),
                device_id_type=MESH,
            ).start()

    @pl.when(section > 0)
    def _():
        spread(widen_s, widen_t, 4, 5)
        spread_own(widen_s, widen_t, 5)

    def adapter_of(index):
        return adapter_ref[lax.div(lax.rem(index, per_micro), BLOCK // CHUNK), lax.div(index, per_micro)]

    def partner_of(colour, phase, mask):
        mask_x, mask_y = (mask, 0) if colour == phase else (0, mask)
        return (flipped(y, mask_y) * RING + flipped(x, mask_x)) * 2 + core

    def colour_rows(colour):
        return pl.ds(colour * (PIECE // 2), PIECE // 2)

    def remote(source, target, send, receive, plane, rank):
        return pltpu.make_async_remote_copy(
            src_ref=source,
            dst_ref=target,
            send_sem=send,
            recv_sem=receive,
            device_id=mesh_id(plane, rank),
            device_id_type=MESH,
        )

    def first_rows(index):
        ring_slot = lax.rem(index, DEPTH)
        return [
            remote(
                gathered.at[index, colour, 0, 0],
                gathered.at[index, colour, 0, mask],
                gs.at[ring_slot, 0, colour, mask - 1],
                gr.at[ring_slot, 0, colour, mask - 1],
                section,
                partner_of(colour, 0, mask),
            )
            for mask in (2, 3, 1)
            for colour in range(COLOURS)
        ]

    def first_sums(index):
        ring_slot = lax.rem(index, DEPTH)
        return [
            remote(
                sums_in.at[index, 0, 0, colour_rows(colour)],
                sums_in.at[index, 0, mask, colour_rows(colour)],
                as_.at[ring_slot, 0, colour, mask - 1],
                ar_.at[ring_slot, 0, colour, mask - 1],
                section,
                partner_of(colour, 0, mask),
            )
            for mask in (2, 3, 1)
            for colour in range(COLOURS)
        ]

    def second_rows(index):
        ring_slot = lax.rem(index, DEPTH)
        return [
            remote(
                gathered.at[index, colour, 0],
                gathered.at[index, colour, mask],
                gs.at[ring_slot, 1, colour, mask - 1],
                gr.at[ring_slot, 1, colour, mask - 1],
                section,
                partner_of(colour, 1, mask),
            )
            for mask in (3, 1)
            for colour in range(COLOURS)
        ]

    def third_rows(index):
        ring_slot = lax.rem(index, DEPTH)
        return [
            remote(
                gathered.at[index, colour, 4 - mask, pl.ds(half, 2)],
                gathered.at[index, colour, 2, pl.ds(half, 2)],
                ts.at[ring_slot, colour, half // 2],
                tr.at[ring_slot, colour, half // 2],
                section,
                partner_of(colour, 1, mask),
            )
            for mask, half in ((1, 0), (3, 2))
            for colour in range(COLOURS)
        ]

    def second_sums(index):
        ring_slot = lax.rem(index, DEPTH)
        return [
            remote(
                sums_out.at[index, colour_rows(colour)],
                sums_in.at[index, 1, mask, colour_rows(colour)],
                as_.at[ring_slot, 1, colour, mask - 1],
                ar_.at[ring_slot, 1, colour, mask - 1],
                section,
                partner_of(colour, 1, mask),
            )
            for mask in (2, 3, 1)
            for colour in range(COLOURS)
        ]

    def forward(index):
        for copy in second_rows(index):
            copy.wait_recv()
        for copy in third_rows(index):
            copy.start()

    def relay(index):
        for copy in first_rows(index):
            copy.wait_recv()
        for copy in second_rows(index):
            copy.start()
        for copy in first_sums(index):
            copy.wait_recv()
        total = sums_in[index, 0, 0].astype(jnp.float32)
        for mask in (1, 2, 3):
            total = total + sums_in[index, 0, mask].astype(jnp.float32)
        running[index] = total
        sums_out[index] = total.astype(jnp.bfloat16)
        for copy in second_sums(index):
            copy.start()

    def finish_gather(index):
        for copy in second_sums(index) + third_rows(index):
            copy.wait_recv()
        total = running[index]
        for mask in (1, 2, 3):
            total = total + sums_in[index, 1, mask].astype(jnp.float32)
        rows = left_side(index).astype(jnp.float32)
        squares = jnp.sum(rows * rows, axis=1, keepdims=True)
        final_sums[index] = jnp.concatenate(
            [unpack(total), jnp.broadcast_to(squares, (CHUNK, LANES - RANK))], axis=1
        )

    def inner_products(h, scale_by, maps):
        scaled = (h.astype(jnp.float32) * scale_by).astype(jnp.bfloat16)
        inner = lax.dot_general(scaled, maps, (((1,), (1,)), ((), ())), preferred_element_type=jnp.float32)
        return pack(inner).astype(jnp.bfloat16)

    def own_rows(index):
        return jnp.concatenate([gathered[index, colour, 0, 0] for colour in range(COLOURS)], axis=0)

    def feed(index):
        for colour in range(COLOURS):
            piece = gathered.at[index, colour, 0, 0]
            pltpu.make_async_copy(piece, piece, zr.at[index, colour]).wait()
        for copy in first_rows(index):
            copy.start()
        sums_in[index, 0, 0] = inner_products(own_rows(index), gain_o[...], narrow_t[adapter_of(index)])
        for copy in first_sums(index):
            copy.start()

    def left_side(index):
        return jnp.concatenate(
            [
                jnp.concatenate([gathered[(index, colour) + slot_of(colour, rel)] for colour in range(COLOURS)], axis=0)
                for rel in range(16)
            ],
            axis=1,
        )

    def swaps(index):
        ring_slot = lax.rem(index, DEPTH)
        sums = pltpu.make_async_remote_copy(
            src_ref=final_sums.at[index],
            dst_ref=sib_sums.at[index],
            send_sem=xs.at[ring_slot, 0],
            recv_sem=xr.at[ring_slot, 0],
            device_id=mesh_id(section, other),
            device_id_type=MESH,
        )
        parts = pltpu.make_async_remote_copy(
            src_ref=part_out.at[index],
            dst_ref=part_in.at[index],
            send_sem=xs.at[ring_slot, 1],
            recv_sem=xr.at[ring_slot, 1],
            device_id=mesh_id(section, other),
            device_id_type=MESH,
        )
        return sums, parts

    def multiply_sibling(index):
        sums, parts = swaps(index)
        sums.start()
        part_out[index] = jnp.dot(left_side(index), w_sib[...], preferred_element_type=jnp.float32)
        parts.start()

    def multiply_own(index):
        own_part[...] = jnp.dot(left_side(index), w_own[...], preferred_element_type=jnp.float32)

    def onward(index):
        ring_slot = lax.rem(index, DEPTH)
        return [
            remote(
                next_h.at[index, pl.ds(colour * PIECE, PIECE)],
                gathered.at[index, colour, 0, 0],
                zo.at[ring_slot, colour],
                zr.at[index, colour],
                section + 1,
                mp,
            )
            for colour in range(COLOURS)
        ]

    def homeward(index):
        home = lax.div(index, per_micro)
        part = lax.rem(index, per_micro)
        return pltpu.make_async_remote_copy(
            src_ref=next_h.at[index],
            dst_ref=finished.at[part],
            send_sem=zs.at[index],
            recv_sem=fr.at[part],
            device_id=mesh_id(home, mp),
            device_id_type=MESH,
        )

    def combine(index):
        sums, parts = swaps(index)
        sums.wait_recv()
        total = final_sums[index] + sib_sums[index]
        squares = total[:, RANK : RANK + 1]
        scale = lax.rsqrt(squares / (WIDTH * 32) + 1e-05)
        inner = total[:, :RANK].astype(jnp.bfloat16)
        delta = jnp.dot(inner, widen_t[adapter_of(index)], preferred_element_type=jnp.float32)
        own = own_part[...] + 2.0 * delta
        parts.wait_recv()
        base = own + part_in[index]
        h = own_rows(index).astype(jnp.float32)
        result = (h + scale * base).astype(jnp.bfloat16)
        next_h[index] = result

        @pl.when(section < 3)
        def _():
            for copy in onward(index):
                copy.start()

        @pl.when(section == 3)
        def _():
            @pl.when(index < 3 * per_micro)
            def _():
                homeward(index).start()

            @pl.when(index >= 3 * per_micro)
            def _():
                part = lax.rem(index, per_micro)
                pltpu.make_async_copy(next_h.at[index], finished.at[part], fr.at[part]).start()

    def retire(index):
        for copy in first_rows(index) + first_sums(index) + second_rows(index) + second_sums(index) + third_rows(index):
            copy.wait_send()
        for copy in swaps(index):
            copy.wait_send()

        @pl.when(section < 3)
        def _():
            for copy in onward(index):
                copy.wait_send()

    full_wait(narrow_t, 7)

    @pl.loop(0, chunks + RETIRE)
    def _(tick):
        @pl.when(tick < chunks)
        def _():
            feed(tick)

        @pl.when(tick == LATE)
        def _():
            part_wait(narrow_t, 6)
            full_wait(widen_t, 5)

            @pl.when(section > 0)
            def _():
                part_wait(widen_t, 4)

            @pl.when(lax.rem(section, 2) == 1)
            def _():
                full_wait(relay_s, 19)

            @pl.when(section == 0)
            def _():
                for half in (0, 1):
                    aside(half).wait_send()

        @pl.when((tick >= LATE) & (tick < chunks + LATE))
        def _():
            finish_gather(tick - LATE)
            multiply_sibling(tick - LATE)

        @pl.when((tick >= 1) & (tick <= chunks))
        def _():
            relay(tick - 1)

        @pl.when((tick >= LATE) & (tick < chunks + LATE))
        def _():
            multiply_own(tick - LATE)
            combine(tick - LATE)

        @pl.when((tick >= 2) & (tick <= chunks + 1))
        def _():
            forward(tick - 2)

        @pl.when(tick >= RETIRE)
        def _():
            retire(tick - RETIRE)

    @pl.when(section > 0)
    def _():
        for part in range(per_micro):
            for colour in range(COLOURS):
                piece = gathered.at[0, colour, 0, 0]
                pltpu.make_async_copy(piece, piece, fs.at[part, colour]).wait()

    @pl.when(section == 3)
    def _():
        @pl.loop(0, 3 * per_micro)
        def _(index):
            pltpu.make_async_copy(next_h.at[index], next_h.at[index], zs.at[index]).wait()

    for part in range(per_micro):
        pltpu.make_async_copy(finished.at[part], finished.at[part], fr.at[part]).wait()
    hidden = jnp.concatenate([finished[part] for part in range(per_micro)], axis=0)
    out_ref[...] = hidden
    head = jnp.broadcast_to(head_ref[...].reshape(1, WIDTH), (8, WIDTH))
    partial = lax.dot_general(head, hidden, (((1,), (1,)), ((), ())), preferred_element_type=jnp.float32)
    score_part[...] = partial[:1]

    def score_send(offset):
        return pltpu.make_async_remote_copy(
            src_ref=score_part,
            dst_ref=score_all.at[mp],
            send_sem=once.at[14],
            recv_sem=once.at[15],
            device_id=mesh_id(section, lax.rem(mp + offset, 32)),
            device_id_type=MESH,
        )

    @pl.loop(1, 32)
    def _(offset):
        score_send(offset).start()

    pltpu.make_async_copy(score_part, score_all.at[mp], once.at[15]).start()
    pltpu.make_async_copy(score_all, score_all, once.at[15]).wait()
    pltpu.make_async_copy(score_all.at[pl.ds(0, 31)], score_all.at[pl.ds(0, 31)], once.at[14]).wait()
    raw = jnp.sum(score_all[...], axis=0)
    place = lax.broadcasted_iota(jnp.int32, (1, 2 * BLOCK), 1)
    limit = jnp.where(place < BLOCK, live_ref[0, 0], live_ref[0, 1])
    score_ref[...] = jnp.where(lax.rem(place, BLOCK) < limit, raw, 0.0)


def shards(
    entering_hidden,
    section_weight,
    section_norm_gain,
    plugin_narrowing_factors,
    plugin_widening_factors,
    reward_head,
    adapter_of_block,
    live_block_rows,
):
    chunks = 1024 // CHUNK
    bf16, f32 = jnp.bfloat16, jnp.float32
    vmem = pl.BlockSpec(memory_space=pltpu.VMEM)
    smem = pl.BlockSpec(memory_space=pltpu.SMEM)
    anywhere = pl.BlockSpec(memory_space=pl.ANY)
    dma = pltpu.SemaphoreType.DMA
    hidden, scores = pl.pallas_call(
        functools.partial(kernel, chunks),
        out_shape=(
            jax.ShapeDtypeStruct((256, WIDTH), bf16),
            jax.ShapeDtypeStruct((1, 256), f32),
        ),
        in_specs=[smem, smem, anywhere, anywhere, vmem, anywhere, anywhere, vmem],
        out_specs=(vmem, vmem),
        scratch_shapes=[
            pltpu.VMEM((chunks, COLOURS, RING, RING, PIECE, WIDTH), bf16),
            pltpu.VMEM((chunks, CHUNK // 2, LANES), bf16),
            pltpu.VMEM((chunks, PHASES, RING, CHUNK // 2, LANES), bf16),
            pltpu.VMEM((chunks, CHUNK // 2, LANES), f32),
            pltpu.VMEM((chunks, CHUNK, LANES), f32),
            pltpu.VMEM((chunks, CHUNK, LANES), f32),
            pltpu.VMEM((chunks, CHUNK, WIDTH), f32),
            pltpu.VMEM((chunks, CHUNK, WIDTH), f32),
            pltpu.VMEM((CHUNK, WIDTH), f32),
            pltpu.VMEM((chunks, CHUNK, WIDTH), bf16),
            pltpu.VMEM((16 * WIDTH, WIDTH), bf16),
            pltpu.VMEM((16 * WIDTH, WIDTH), bf16),
            pltpu.VMEM((32, RANK, WIDTH), bf16),
            pltpu.VMEM((32, RANK, WIDTH), bf16),
            pltpu.VMEM((16, RANK, WIDTH), bf16),
            pltpu.VMEM((32, RANK, WIDTH), bf16),
            pltpu.VMEM((32, RANK, WIDTH), bf16),
            pltpu.VMEM((1, WIDTH), f32),
            pltpu.VMEM((16, 1, WIDTH), f32),
            pltpu.VMEM((256 // CHUNK, CHUNK, WIDTH), bf16),
            pltpu.VMEM((1, 256), f32),
            pltpu.VMEM((32, 1, 256), f32),
            dma((DEPTH, PHASES, COLOURS, 3)),
            dma((DEPTH, PHASES, COLOURS, 3)),
            dma((DEPTH, PHASES, COLOURS, 3)),
            dma((DEPTH, PHASES, COLOURS, 3)),
            dma((DEPTH, COLOURS, 2)),
            dma((DEPTH, COLOURS, 2)),
            dma((DEPTH, 2)),
            dma((DEPTH, 2)),
            dma((chunks,)),
            dma((DEPTH, COLOURS)),
            dma((chunks, COLOURS)),
            dma((4, COLOURS)),
            dma((4,)),
            dma((20,)),
        ],
        compiler_params=pltpu.CompilerParams(
            collective_id=0, has_side_effects=True, vmem_limit_bytes=60 * 1024 * 1024
        ),
    )(
        adapter_of_block.T,
        live_block_rows,
        entering_hidden[0],
        section_weight[0],
        section_norm_gain,
        plugin_narrowing_factors[0, 0].T,
        plugin_widening_factors[0, 0],
        reward_head,
    )
    return hidden[None], scores


def solution(mesh):
    placed = (
        P("section", None, "mp"),
        P("section", None, "mp"),
        P("section", "mp"),
        P("section", "mp", None, None),
        P("section", "mp", None, None),
        P("mp"),
        P(),
        P("section", None),
    )
    return jax.shard_map(
        shards,
        mesh=mesh,
        in_specs=placed,
        out_specs=(P("section", None, "mp"), P("section", None)),
        check_vma=False,
    )
```

```python
import functools

import jax
import jax.numpy as jnp
from jax import lax
from jax.experimental import pallas as pl
from jax.experimental.pallas import tpu as pltpu
from jax.sharding import PartitionSpec as P

MESH = pl.DeviceIdType.MESH
BLOCK = 128
CHUNK = 64
COLOURS = 2
PHASES = 2
PIECE = CHUNK // COLOURS
RING = 4
WIDTH = 256
RANK = 64
LANES = 128
LATE = 4
EARLY = 2
RETIRE = 5
DEPTH = 6

FAR = ((2, 2), (3, 2), (2, 3), (1, 2), (2, 1), (0, 2), (2, 0), (3, 1), (1, 3), (3, 3), (1, 1), (0, 3), (3, 0), (0, 1), (1, 0))


def flipped(position, mask):
    if mask == 0:
        return position
    if mask == 1:
        return position + 1 - 2 * lax.rem(position, 2)
    if mask == 2:
        return lax.rem(position + 2, 4)
    return 3 - position


def slot_of(colour, rel):
    return (rel // 4, rel % 4) if colour == 0 else (rel % 4, rel // 4)


def pack(value):
    pieces = []
    for colour in range(COLOURS):
        first = colour * PIECE
        pieces.append(
            jnp.concatenate([value[first : first + PIECE // 2], value[first + PIECE // 2 : first + PIECE]], axis=1)
        )
    return jnp.concatenate(pieces, axis=0)


def unpack(value):
    pieces = []
    for colour in range(COLOURS):
        piece = value[colour * PIECE // 2 : (colour + 1) * PIECE // 2]
        pieces += [piece[:, :RANK], piece[:, RANK:]]
    return jnp.concatenate(pieces, axis=0)


def kernel(
    chunks,
    adapter_ref,
    live_ref,
    enter_ref,
    weight_ref,
    gain_ref,
    narrow_ref,
    widen_ref,
    head_ref,
    out_ref,
    score_ref,
    gathered,
    sums_out,
    sums_in,
    running,
    final_sums,
    sib_sums,
    part_out,
    part_in,
    own_part,
    next_h,
    w_own,
    w_sib,
    narrow_s,
    widen_s,
    relay_s,
    narrow_t,
    widen_t,
    gain_o,
    gains,
    finished,
    score_part,
    score_all,
    gs,
    gr,
    as_,
    ar_,
    ts,
    tr,
    xs,
    xr,
    zs,
    zo,
    zr,
    fs,
    fr,
    once,
):
    section = lax.axis_index("section")
    mp = lax.axis_index("mp")
    core = lax.rem(mp, 2)
    chip = lax.div(mp, 2)
    x = lax.rem(chip, RING)
    y = lax.div(chip, RING)
    other = mp + 1 - 2 * core
    per_micro = 256 // CHUNK

    def mesh_id(where, rank):
        return {"section": where, "mp": rank}

    barrier = pltpu.get_barrier_semaphore()
    plane_ranks = [
        (flipped(y, mask_y) * RING + flipped(x, mask_x)) * 2 + (1 - core if flip else core)
        for mask_x, mask_y in FAR + ((0, 0),)
        for flip in (0, 1)
        if flip or mask_x or mask_y
    ]
    for rank in plane_ranks:
        pl.semaphore_signal(barrier, inc=1, device_id=mesh_id(section, rank), device_id_type=MESH)
    for offset in range(1, 4):
        pl.semaphore_signal(
            barrier, inc=1, device_id=mesh_id(lax.rem(section + offset, 4), mp), device_id_type=MESH
        )

    def chip_of(rel):
        return flipped(y, rel // 4) * RING + flipped(x, rel % 4)

    for rel in range(16):
        rows = pl.ds(pl.multiple_of((chip_of(rel) * 2 + core) * WIDTH, WIDTH), WIDTH)
        pltpu.make_async_copy(
            weight_ref.at[rows], w_own.at[pl.ds(rel * WIDTH, WIDTH)], once.at[1]
        ).start()

    def columns(rank):
        return pl.ds(pl.multiple_of(rank * WIDTH, WIDTH), WIDTH)

    def stage(rank):
        return lax.rem(rank, 2) * 16 + lax.div(rank, 2)

    for rank in range(32):
        slot = rank % 2 * 16 + rank // 2
        pltpu.make_async_copy(narrow_ref.at[:, columns(rank)], narrow_s.at[slot], once.at[0]).start()
        pltpu.make_async_copy(widen_ref.at[:, columns(rank)], widen_s.at[slot], once.at[10]).start()

    @pl.when(section == 0)
    def _():
        for part in range(per_micro):
            for colour in range(COLOURS):
                pltpu.make_async_copy(
                    enter_ref.at[pl.ds(part * CHUNK + colour * PIECE, PIECE)],
                    gathered.at[part, colour, 0, 0],
                    zr.at[part, colour],
                ).start()

    pl.semaphore_wait(barrier, 34)

    @pl.when(section > 0)
    def _():
        for part in range(per_micro):
            index = section * per_micro + part
            for colour in range(COLOURS):
                pltpu.make_async_remote_copy(
                    src_ref=enter_ref.at[pl.ds(part * CHUNK + colour * PIECE, PIECE)],
                    dst_ref=gathered.at[index, colour, 0, 0],
                    send_sem=fs.at[part, colour],
                    recv_sem=zr.at[index, colour],
                    device_id=mesh_id(0, mp),
                    device_id_type=MESH,
                ).start()

    def swap_weight(rel):
        rows = pl.ds(pl.multiple_of((chip_of(rel) * 2 + 1 - core) * WIDTH, WIDTH), WIDTH)
        return pltpu.make_async_remote_copy(
            src_ref=weight_ref.at[rows],
            dst_ref=w_sib.at[pl.ds(rel * WIDTH, WIDTH)],
            send_sem=once.at[2],
            recv_sem=once.at[3],
            device_id=mesh_id(section, other),
            device_id_type=MESH,
        )

    def spread(source, table, send, receive):
        for other_core in (0, 1):
            for mask_x, mask_y in FAR + (((0, 0),) if other_core else ()):
                rank = (flipped(y, mask_y) * RING + flipped(x, mask_x)) * 2 + (1 - core if other_core else core)
                pltpu.make_async_remote_copy(
                    src_ref=source.at[stage(rank)],
                    dst_ref=table.at[mp],
                    send_sem=once.at[send],
                    recv_sem=once.at[receive],
                    device_id=mesh_id(section, rank),
                    device_id_type=MESH,
                ).start()

    def spread_own(source, table, receive):
        pltpu.make_async_copy(source.at[stage(mp)], table.at[mp], once.at[receive]).start()

    def full_wait(table, semaphore):
        pltpu.make_async_copy(table, table, once.at[semaphore]).wait()

    def part_wait(table, semaphore):
        part = table.at[pl.ds(0, 31)]
        pltpu.make_async_copy(part, part, once.at[semaphore]).wait()

    full_wait(widen_s, 10)

    def aside(half):
        return pltpu.make_async_remote_copy(
            src_ref=widen_s.at[pl.ds(half * 16, 16)],
            dst_ref=relay_s,
            send_sem=once.at[16 + half],
            recv_sem=once.at[18],
            device_id=mesh_id(2 * half + 1, mp),
            device_id_type=MESH,
        )

    @pl.when(section == 0)
    def _():
        for half in (0, 1):
            aside(half).start()

    def partner_of(colour, phase, mask):
        mask_x, mask_y = (mask, 0) if colour == phase else (0, mask)
        return (flipped(y, mask_y) * RING + flipped(x, mask_x)) * 2 + core

    def colour_rows(colour):
        return pl.ds(colour * (PIECE // 2), PIECE // 2)

    def remote(source, target, send, receive, plane, rank):
        return pltpu.make_async_remote_copy(
            src_ref=source,
            dst_ref=target,
            send_sem=send,
            recv_sem=receive,
            device_id=mesh_id(plane, rank),
            device_id_type=MESH,
        )

    def first_rows(index):
        ring_slot = lax.rem(index, DEPTH)
        return [
            remote(
                gathered.at[index, colour, 0, 0],
                gathered.at[index, colour, 0, mask],
                gs.at[ring_slot, 0, colour, mask - 1],
                gr.at[ring_slot, 0, colour, mask - 1],
                section,
                partner_of(colour, 0, mask),
            )
            for mask in (2, 3, 1)
            for colour in range(COLOURS)
        ]

    def feed_rows(index):
        leaving = first_rows(index)
        for colour in range(COLOURS):
            piece = gathered.at[index, colour, 0, 0]
            pltpu.make_async_copy(piece, piece, zr.at[index, colour]).wait()
            for copy in leaving[colour::COLOURS]:
                copy.start()

    @pl.when(section == 0)
    def _():
        for index in range(EARLY):
            feed_rows(index)

    full_wait(narrow_s, 0)
    spread(narrow_s, narrow_t, 6, 7)
    spread_own(narrow_s, narrow_t, 7)

    for rel in range(16):
        swap_weight(rel).start()
    gain_o[...] = gain_ref[...].astype(jnp.float32)
    for mask_x, mask_y in FAR:
        pltpu.make_async_remote_copy(
            src_ref=gain_o,
            dst_ref=gains.at[mask_y * RING + mask_x],
            send_sem=once.at[8],
            recv_sem=once.at[9],
            device_id=mesh_id(section, (flipped(y, mask_y) * RING + flipped(x, mask_x)) * 2 + core),
            device_id_type=MESH,
        ).start()
    pltpu.make_async_copy(gain_o, gains.at[0], once.at[9]).start()

    def fold_gains():
        full_wait(w_own, 1)
        full_wait(w_sib, 3)
        full_wait(w_sib, 2)
        full_wait(gains, 9)
        pltpu.make_async_copy(gains.at[pl.ds(0, 15)], gains.at[pl.ds(0, 15)], once.at[8]).wait()

        @pl.loop(0, 16)
        def _(rel):
            rows = pl.ds(pl.multiple_of(rel * WIDTH, WIDTH), WIDTH)
            diagonal = lax.broadcasted_iota(jnp.int32, (WIDTH, WIDTH), 0) == lax.broadcasted_iota(
                jnp.int32, (WIDTH, WIDTH), 1
            )
            factor = jnp.sum(jnp.where(diagonal, gains[rel], 0.0), axis=1, keepdims=True)
            w_own[rows] = (w_own[rows].astype(jnp.float32) * factor).astype(jnp.bfloat16)
            w_sib[rows] = (w_sib[rows].astype(jnp.float32) * factor).astype(jnp.bfloat16)

    fold_gains()

    @pl.when(lax.rem(section, 2) == 1)
    def _():
        full_wait(relay_s, 18)
        for mask_x, mask_y in FAR + ((0, 0),):
            target = flipped(y, mask_y) * RING + flipped(x, mask_x)
            pltpu.make_async_remote_copy(
                src_ref=relay_s.at[target],
                dst_ref=widen_t.at[mp],
                send_sem=once.at[19],
                recv_sem=once.at[5],
                device_id=mesh_id(0, target * 2 + lax.div(section, 2)),
                device_id_type=MESH,
            ).start()

    @pl.when(section > 0)
    def _():
        spread(widen_s, widen_t, 4, 5)
        spread_own(widen_s, widen_t, 5)

    def adapter_of(index):
        return adapter_ref[lax.div(lax.rem(index, per_micro), BLOCK // CHUNK), lax.div(index, per_micro)]

    def first_sums(index):
        ring_slot = lax.rem(index, DEPTH)
        return [
            remote(
                sums_in.at[index, 0, 0, colour_rows(colour)],
                sums_in.at[index, 0, mask, colour_rows(colour)],
                as_.at[ring_slot, 0, colour, mask - 1],
                ar_.at[ring_slot, 0, colour, mask - 1],
                section,
                partner_of(colour, 0, mask),
            )
            for mask in (2, 3, 1)
            for colour in range(COLOURS)
        ]

    def second_rows(index):
        ring_slot = lax.rem(index, DEPTH)
        return [
            remote(
                gathered.at[index, colour, 0],
                gathered.at[index, colour, mask],
                gs.at[ring_slot, 1, colour, mask - 1],
                gr.at[ring_slot, 1, colour, mask - 1],
                section,
                partner_of(colour, 1, mask),
            )
            for mask in (3, 1)
            for colour in range(COLOURS)
        ]

    def third_rows(index):
        ring_slot = lax.rem(index, DEPTH)
        return [
            remote(
                gathered.at[index, colour, 4 - mask, pl.ds(half, 2)],
                gathered.at[index, colour, 2, pl.ds(half, 2)],
                ts.at[ring_slot, colour, half // 2],
                tr.at[ring_slot, colour, half // 2],
                section,
                partner_of(colour, 1, mask),
            )
            for mask, half in ((1, 0), (3, 2))
            for colour in range(COLOURS)
        ]

    def second_sums(index):
        ring_slot = lax.rem(index, DEPTH)
        return [
            remote(
                sums_out.at[index, colour_rows(colour)],
                sums_in.at[index, 1, mask, colour_rows(colour)],
                as_.at[ring_slot, 1, colour, mask - 1],
                ar_.at[ring_slot, 1, colour, mask - 1],
                section,
                partner_of(colour, 1, mask),
            )
            for mask in (2, 3, 1)
            for colour in range(COLOURS)
        ]

    def forward(index):
        for arriving, leaving in zip(second_rows(index), third_rows(index)):
            arriving.wait_recv()
            leaving.start()

    def relay(index):
        arriving, leaving = first_rows(index), second_rows(index)
        for colour in range(COLOURS):
            for copy in arriving[colour::COLOURS]:
                copy.wait_recv()
            for copy in leaving[colour::COLOURS]:
                copy.start()
        for copy in first_sums(index):
            copy.wait_recv()
        total = sums_in[index, 0, 0].astype(jnp.float32)
        for mask in (1, 2, 3):
            total = total + sums_in[index, 0, mask].astype(jnp.float32)
        running[index] = total
        sums_out[index] = total.astype(jnp.bfloat16)
        for copy in second_sums(index):
            copy.start()

    def finish_gather(index):
        for copy in second_sums(index) + third_rows(index):
            copy.wait_recv()
        total = running[index]
        for mask in (1, 2, 3):
            total = total + sums_in[index, 1, mask].astype(jnp.float32)
        rows = left_side(index).astype(jnp.float32)
        squares = jnp.sum(rows * rows, axis=1, keepdims=True)
        final_sums[index] = jnp.concatenate(
            [unpack(total), jnp.broadcast_to(squares, (CHUNK, LANES - RANK))], axis=1
        )

    def inner_products(h, scale_by, maps):
        scaled = (h.astype(jnp.float32) * scale_by).astype(jnp.bfloat16)
        inner = lax.dot_general(scaled, maps, (((1,), (1,)), ((), ())), preferred_element_type=jnp.float32)
        return pack(inner).astype(jnp.bfloat16)

    def own_rows(index):
        return jnp.concatenate([gathered[index, colour, 0, 0] for colour in range(COLOURS)], axis=0)

    def feed_sums(index):
        sums_in[index, 0, 0] = inner_products(own_rows(index), gain_o[...], narrow_t[adapter_of(index)])
        for copy in first_sums(index):
            copy.start()

    def left_side(index):
        return jnp.concatenate(
            [
                jnp.concatenate([gathered[(index, colour) + slot_of(colour, rel)] for colour in range(COLOURS)], axis=0)
                for rel in range(16)
            ],
            axis=1,
        )

    def swaps(index):
        ring_slot = lax.rem(index, DEPTH)
        sums = pltpu.make_async_remote_copy(
            src_ref=final_sums.at[index],
            dst_ref=sib_sums.at[index],
            send_sem=xs.at[ring_slot, 0],
            recv_sem=xr.at[ring_slot, 0],
            device_id=mesh_id(section, other),
            device_id_type=MESH,
        )
        parts = pltpu.make_async_remote_copy(
            src_ref=part_out.at[index],
            dst_ref=part_in.at[index],
            send_sem=xs.at[ring_slot, 1],
            recv_sem=xr.at[ring_slot, 1],
            device_id=mesh_id(section, other),
            device_id_type=MESH,
        )
        return sums, parts

    def multiply_sibling(index):
        sums, parts = swaps(index)
        sums.start()
        part_out[index] = jnp.dot(left_side(index), w_sib[...], preferred_element_type=jnp.float32)
        parts.start()

    def multiply_own(index):
        own_part[...] = jnp.dot(left_side(index), w_own[...], preferred_element_type=jnp.float32)

    def onward(index):
        ring_slot = lax.rem(index, DEPTH)
        return [
            remote(
                next_h.at[index, pl.ds(colour * PIECE, PIECE)],
                gathered.at[index, colour, 0, 0],
                zo.at[ring_slot, colour],
                zr.at[index, colour],
                section + 1,
                mp,
            )
            for colour in range(COLOURS)
        ]

    def homeward(index):
        home = lax.div(index, per_micro)
        part = lax.rem(index, per_micro)
        return pltpu.make_async_remote_copy(
            src_ref=next_h.at[index],
            dst_ref=finished.at[part],
            send_sem=zs.at[index],
            recv_sem=fr.at[part],
            device_id=mesh_id(home, mp),
            device_id_type=MESH,
        )

    def combine(index):
        sums, parts = swaps(index)
        sums.wait_recv()
        total = final_sums[index] + sib_sums[index]
        squares = total[:, RANK : RANK + 1]
        scale = lax.rsqrt(squares / (WIDTH * 32) + 1e-05)
        inner = total[:, :RANK].astype(jnp.bfloat16)
        delta = jnp.dot(inner, widen_t[adapter_of(index)], preferred_element_type=jnp.float32)
        own = own_part[...] + 2.0 * delta
        parts.wait_recv()
        base = own + part_in[index]
        h = own_rows(index).astype(jnp.float32)
        result = (h + scale * base).astype(jnp.bfloat16)
        next_h[index] = result

        @pl.when(section < 3)
        def _():
            for copy in onward(index):
                copy.start()

        @pl.when(section == 3)
        def _():
            @pl.when(index < 3 * per_micro)
            def _():
                homeward(index).start()

            @pl.when(index >= 3 * per_micro)
            def _():
                part = lax.rem(index, per_micro)
                pltpu.make_async_copy(next_h.at[index], finished.at[part], fr.at[part]).start()

    def retire(index):
        for copy in first_rows(index) + first_sums(index) + second_rows(index) + second_sums(index) + third_rows(index):
            copy.wait_send()
        for copy in swaps(index):
            copy.wait_send()

        @pl.when(section < 3)
        def _():
            for copy in onward(index):
                copy.wait_send()

    full_wait(narrow_t, 7)

    @pl.loop(0, chunks + RETIRE)
    def _(tick):
        @pl.when(tick < chunks)
        def _():
            @pl.when((section > 0) | (tick >= EARLY))
            def _():
                feed_rows(tick)

            feed_sums(tick)

        @pl.when(tick == LATE)
        def _():
            part_wait(narrow_t, 6)
            full_wait(widen_t, 5)

            @pl.when(section > 0)
            def _():
                part_wait(widen_t, 4)

            @pl.when(lax.rem(section, 2) == 1)
            def _():
                full_wait(relay_s, 19)

            @pl.when(section == 0)
            def _():
                for half in (0, 1):
                    aside(half).wait_send()

        @pl.when((tick >= LATE) & (tick < chunks + LATE))
        def _():
            finish_gather(tick - LATE)
            multiply_sibling(tick - LATE)

        @pl.when((tick >= 1) & (tick <= chunks))
        def _():
            relay(tick - 1)

        @pl.when((tick >= LATE) & (tick < chunks + LATE))
        def _():
            multiply_own(tick - LATE)
            combine(tick - LATE)

        @pl.when((tick >= 2) & (tick <= chunks + 1))
        def _():
            forward(tick - 2)

        @pl.when(tick >= RETIRE)
        def _():
            retire(tick - RETIRE)

    @pl.when(section > 0)
    def _():
        for part in range(per_micro):
            for colour in range(COLOURS):
                piece = gathered.at[0, colour, 0, 0]
                pltpu.make_async_copy(piece, piece, fs.at[part, colour]).wait()

    @pl.when(section == 3)
    def _():
        @pl.loop(0, 3 * per_micro)
        def _(index):
            pltpu.make_async_copy(next_h.at[index], next_h.at[index], zs.at[index]).wait()

    for part in range(per_micro):
        pltpu.make_async_copy(finished.at[part], finished.at[part], fr.at[part]).wait()
    hidden = jnp.concatenate([finished[part] for part in range(per_micro)], axis=0)
    out_ref[...] = hidden
    head = jnp.broadcast_to(head_ref[...].reshape(1, WIDTH), (8, WIDTH))
    partial = lax.dot_general(head, hidden, (((1,), (1,)), ((), ())), preferred_element_type=jnp.float32)
    score_part[...] = partial[:1]

    for rank in plane_ranks:
        pltpu.make_async_remote_copy(
            src_ref=score_part,
            dst_ref=score_all.at[mp],
            send_sem=once.at[14],
            recv_sem=once.at[15],
            device_id=mesh_id(section, rank),
            device_id_type=MESH,
        ).start()

    pltpu.make_async_copy(score_part, score_all.at[mp], once.at[15]).start()
    pltpu.make_async_copy(score_all, score_all, once.at[15]).wait()
    pltpu.make_async_copy(score_all.at[pl.ds(0, 31)], score_all.at[pl.ds(0, 31)], once.at[14]).wait()
    raw = jnp.sum(score_all[...], axis=0)
    place = lax.broadcasted_iota(jnp.int32, (1, 2 * BLOCK), 1)
    limit = jnp.where(place < BLOCK, live_ref[0, 0], live_ref[0, 1])
    score_ref[...] = jnp.where(lax.rem(place, BLOCK) < limit, raw, 0.0)


def shards(
    entering_hidden,
    section_weight,
    section_norm_gain,
    plugin_narrowing_factors,
    plugin_widening_factors,
    reward_head,
    adapter_of_block,
    live_block_rows,
):
    chunks = 1024 // CHUNK
    bf16, f32 = jnp.bfloat16, jnp.float32
    vmem = pl.BlockSpec(memory_space=pltpu.VMEM)
    smem = pl.BlockSpec(memory_space=pltpu.SMEM)
    anywhere = pl.BlockSpec(memory_space=pl.ANY)
    dma = pltpu.SemaphoreType.DMA
    hidden, scores = pl.pallas_call(
        functools.partial(kernel, chunks),
        out_shape=(
            jax.ShapeDtypeStruct((256, WIDTH), bf16),
            jax.ShapeDtypeStruct((1, 256), f32),
        ),
        in_specs=[smem, smem, anywhere, anywhere, vmem, anywhere, anywhere, vmem],
        out_specs=(vmem, vmem),
        scratch_shapes=[
            pltpu.VMEM((chunks, COLOURS, RING, RING, PIECE, WIDTH), bf16),
            pltpu.VMEM((chunks, CHUNK // 2, LANES), bf16),
            pltpu.VMEM((chunks, PHASES, RING, CHUNK // 2, LANES), bf16),
            pltpu.VMEM((chunks, CHUNK // 2, LANES), f32),
            pltpu.VMEM((chunks, CHUNK, LANES), f32),
            pltpu.VMEM((chunks, CHUNK, LANES), f32),
            pltpu.VMEM((chunks, CHUNK, WIDTH), f32),
            pltpu.VMEM((chunks, CHUNK, WIDTH), f32),
            pltpu.VMEM((CHUNK, WIDTH), f32),
            pltpu.VMEM((chunks, CHUNK, WIDTH), bf16),
            pltpu.VMEM((16 * WIDTH, WIDTH), bf16),
            pltpu.VMEM((16 * WIDTH, WIDTH), bf16),
            pltpu.VMEM((32, RANK, WIDTH), bf16),
            pltpu.VMEM((32, RANK, WIDTH), bf16),
            pltpu.VMEM((16, RANK, WIDTH), bf16),
            pltpu.VMEM((32, RANK, WIDTH), bf16),
            pltpu.VMEM((32, RANK, WIDTH), bf16),
            pltpu.VMEM((1, WIDTH), f32),
            pltpu.VMEM((16, 1, WIDTH), f32),
            pltpu.VMEM((256 // CHUNK, CHUNK, WIDTH), bf16),
            pltpu.VMEM((1, 256), f32),
            pltpu.VMEM((32, 1, 256), f32),
            dma((DEPTH, PHASES, COLOURS, 3)),
            dma((DEPTH, PHASES, COLOURS, 3)),
            dma((DEPTH, PHASES, COLOURS, 3)),
            dma((DEPTH, PHASES, COLOURS, 3)),
            dma((DEPTH, COLOURS, 2)),
            dma((DEPTH, COLOURS, 2)),
            dma((DEPTH, 2)),
            dma((DEPTH, 2)),
            dma((chunks,)),
            dma((DEPTH, COLOURS)),
            dma((chunks, COLOURS)),
            dma((4, COLOURS)),
            dma((4,)),
            dma((20,)),
        ],
        compiler_params=pltpu.CompilerParams(
            collective_id=0, has_side_effects=True, vmem_limit_bytes=60 * 1024 * 1024
        ),
    )(
        adapter_of_block.T,
        live_block_rows,
        entering_hidden[0],
        section_weight[0],
        section_norm_gain,
        plugin_narrowing_factors[0, 0].T,
        plugin_widening_factors[0, 0],
        reward_head,
    )
    return hidden[None], scores


def solution(mesh):
    placed = (
        P("section", None, "mp"),
        P("section", None, "mp"),
        P("section", "mp"),
        P("section", "mp", None, None),
        P("section", "mp", None, None),
        P("mp"),
        P(),
        P("section", None),
    )
    return jax.shard_map(
        shards,
        mesh=mesh,
        in_specs=placed,
        out_specs=(P("section", None, "mp"), P("section", None)),
        check_vma=False,
    )
```

```python
import functools

import jax
import jax.numpy as jnp
from jax import lax
from jax.experimental import pallas as pl
from jax.experimental.pallas import tpu as pltpu
from jax.sharding import PartitionSpec as P

MESH = pl.DeviceIdType.MESH
BLOCK = 128
CHUNK = 64
COLOURS = 2
PHASES = 2
PIECE = CHUNK // COLOURS
RING = 4
WIDTH = 256
RANK = 64
LANES = 128
LATE = 4
EARLY = 2
RETIRE = 5
DEPTH = 6

FAR = ((2, 2), (3, 2), (2, 3), (1, 2), (2, 1), (0, 2), (2, 0), (3, 1), (1, 3), (3, 3), (1, 1), (0, 3), (3, 0), (0, 1), (1, 0))


def flipped(position, mask):
    if mask == 0:
        return position
    if mask == 1:
        return position + 1 - 2 * lax.rem(position, 2)
    if mask == 2:
        return lax.rem(position + 2, 4)
    return 3 - position


def slot_of(colour, rel):
    return (rel // 4, rel % 4) if colour == 0 else (rel % 4, rel // 4)


def pack(value):
    pieces = []
    for colour in range(COLOURS):
        first = colour * PIECE
        pieces.append(
            jnp.concatenate([value[first : first + PIECE // 2], value[first + PIECE // 2 : first + PIECE]], axis=1)
        )
    return jnp.concatenate(pieces, axis=0)


def unpack(value):
    pieces = []
    for colour in range(COLOURS):
        piece = value[colour * PIECE // 2 : (colour + 1) * PIECE // 2]
        pieces += [piece[:, :RANK], piece[:, RANK:]]
    return jnp.concatenate(pieces, axis=0)


def kernel(
    chunks,
    adapter_ref,
    live_ref,
    enter_ref,
    weight_ref,
    gain_ref,
    narrow_ref,
    widen_ref,
    head_ref,
    out_ref,
    score_ref,
    gathered,
    sums_out,
    sums_in,
    running,
    final_sums,
    sib_sums,
    part_out,
    part_in,
    own_part,
    next_h,
    w_own,
    w_sib,
    narrow_s,
    widen_s,
    relay_s,
    narrow_t,
    widen_t,
    gain_o,
    gains,
    finished,
    score_part,
    score_all,
    gs,
    gr,
    as_,
    ar_,
    ts,
    tr,
    xs,
    xr,
    zs,
    zo,
    zr,
    fs,
    fr,
    once,
):
    section = lax.axis_index("section")
    mp = lax.axis_index("mp")
    core = lax.rem(mp, 2)
    chip = lax.div(mp, 2)
    x = lax.rem(chip, RING)
    y = lax.div(chip, RING)
    other = mp + 1 - 2 * core
    per_micro = 256 // CHUNK

    def mesh_id(where, rank):
        return {"section": where, "mp": rank}

    barrier = pltpu.get_barrier_semaphore()
    plane_ranks = [
        (flipped(y, mask_y) * RING + flipped(x, mask_x)) * 2 + (1 - core if flip else core)
        for mask_x, mask_y in FAR + ((0, 0),)
        for flip in (0, 1)
        if flip or mask_x or mask_y
    ]
    for rank in plane_ranks:
        pl.semaphore_signal(barrier, inc=1, device_id=mesh_id(section, rank), device_id_type=MESH)
    for offset in range(1, 4):
        pl.semaphore_signal(
            barrier, inc=1, device_id=mesh_id(lax.rem(section + offset, 4), mp), device_id_type=MESH
        )

    def chip_of(rel):
        return flipped(y, rel // 4) * RING + flipped(x, rel % 4)

    for rel in range(16):
        rows = pl.ds(pl.multiple_of((chip_of(rel) * 2 + core) * WIDTH, WIDTH), WIDTH)
        pltpu.make_async_copy(
            weight_ref.at[rows], w_own.at[pl.ds(rel * WIDTH, WIDTH)], once.at[1]
        ).start()

    def columns(rank):
        return pl.ds(pl.multiple_of(rank * WIDTH, WIDTH), WIDTH)

    def stage(rank):
        return lax.rem(rank, 2) * 16 + lax.div(rank, 2)

    for rank in range(32):
        slot = rank % 2 * 16 + rank // 2
        pltpu.make_async_copy(narrow_ref.at[:, columns(rank)], narrow_s.at[slot], once.at[0]).start()
        pltpu.make_async_copy(widen_ref.at[:, columns(rank)], widen_s.at[slot], once.at[10]).start()

    @pl.when(section == 0)
    def _():
        for part in range(per_micro):
            for colour in range(COLOURS):
                pltpu.make_async_copy(
                    enter_ref.at[pl.ds(part * CHUNK + colour * PIECE, PIECE)],
                    gathered.at[part, colour, 0, 0],
                    zr.at[part, colour],
                ).start()

    pl.semaphore_wait(barrier, 34)

    @pl.when(section > 0)
    def _():
        for part in range(per_micro):
            index = section * per_micro + part
            for colour in range(COLOURS):
                pltpu.make_async_remote_copy(
                    src_ref=enter_ref.at[pl.ds(part * CHUNK + colour * PIECE, PIECE)],
                    dst_ref=gathered.at[index, colour, 0, 0],
                    send_sem=fs.at[part, colour],
                    recv_sem=zr.at[index, colour],
                    device_id=mesh_id(0, mp),
                    device_id_type=MESH,
                ).start()

    def swap_weight(rel):
        rows = pl.ds(pl.multiple_of((chip_of(rel) * 2 + 1 - core) * WIDTH, WIDTH), WIDTH)
        return pltpu.make_async_remote_copy(
            src_ref=weight_ref.at[rows],
            dst_ref=w_sib.at[pl.ds(rel * WIDTH, WIDTH)],
            send_sem=once.at[2],
            recv_sem=once.at[3],
            device_id=mesh_id(section, other),
            device_id_type=MESH,
        )

    def spread(source, table, send, receive):
        for other_core in (0, 1):
            for mask_x, mask_y in FAR + (((0, 0),) if other_core else ()):
                rank = (flipped(y, mask_y) * RING + flipped(x, mask_x)) * 2 + (1 - core if other_core else core)
                pltpu.make_async_remote_copy(
                    src_ref=source.at[stage(rank)],
                    dst_ref=table.at[mp],
                    send_sem=once.at[send],
                    recv_sem=once.at[receive],
                    device_id=mesh_id(section, rank),
                    device_id_type=MESH,
                ).start()

    def spread_own(source, table, receive):
        pltpu.make_async_copy(source.at[stage(mp)], table.at[mp], once.at[receive]).start()

    def full_wait(table, semaphore):
        pltpu.make_async_copy(table, table, once.at[semaphore]).wait()

    def part_wait(table, semaphore):
        part = table.at[pl.ds(0, 31)]
        pltpu.make_async_copy(part, part, once.at[semaphore]).wait()

    full_wait(widen_s, 10)

    def aside(half):
        return pltpu.make_async_remote_copy(
            src_ref=widen_s.at[pl.ds(half * 16, 16)],
            dst_ref=relay_s,
            send_sem=once.at[16 + half],
            recv_sem=once.at[18],
            device_id=mesh_id(2 * half + 1, mp),
            device_id_type=MESH,
        )

    @pl.when(section == 0)
    def _():
        for half in (0, 1):
            aside(half).start()

    def partner_of(colour, phase, mask):
        mask_x, mask_y = (mask, 0) if colour == phase else (0, mask)
        return (flipped(y, mask_y) * RING + flipped(x, mask_x)) * 2 + core

    def colour_rows(colour):
        return pl.ds(colour * (PIECE // 2), PIECE // 2)

    def remote(source, target, send, receive, plane, rank):
        return pltpu.make_async_remote_copy(
            src_ref=source,
            dst_ref=target,
            send_sem=send,
            recv_sem=receive,
            device_id=mesh_id(plane, rank),
            device_id_type=MESH,
        )

    def first_rows(index):
        ring_slot = lax.rem(index, DEPTH)
        return [
            remote(
                gathered.at[index, colour, 0, 0],
                gathered.at[index, colour, 0, mask],
                gs.at[ring_slot, 0, colour, mask - 1],
                gr.at[ring_slot, 0, colour, mask - 1],
                section,
                partner_of(colour, 0, mask),
            )
            for mask in (2, 3, 1)
            for colour in range(COLOURS)
        ]

    def feed_rows(index):
        leaving = first_rows(index)
        for colour in range(COLOURS):
            piece = gathered.at[index, colour, 0, 0]
            pltpu.make_async_copy(piece, piece, zr.at[index, colour]).wait()
            for copy in leaving[colour::COLOURS]:
                copy.start()

    @pl.when(section == 0)
    def _():
        for index in range(EARLY):
            feed_rows(index)

    full_wait(narrow_s, 0)
    spread(narrow_s, narrow_t, 6, 7)
    spread_own(narrow_s, narrow_t, 7)

    for rel in range(16):
        swap_weight(rel).start()
    gain_o[...] = gain_ref[...].astype(jnp.float32)
    for mask_x, mask_y in FAR:
        pltpu.make_async_remote_copy(
            src_ref=gain_o,
            dst_ref=gains.at[mask_y * RING + mask_x],
            send_sem=once.at[8],
            recv_sem=once.at[9],
            device_id=mesh_id(section, (flipped(y, mask_y) * RING + flipped(x, mask_x)) * 2 + core),
            device_id_type=MESH,
        ).start()
    pltpu.make_async_copy(gain_o, gains.at[0], once.at[9]).start()

    def fold_gains():
        full_wait(w_own, 1)
        full_wait(w_sib, 3)
        full_wait(w_sib, 2)
        full_wait(gains, 9)
        pltpu.make_async_copy(gains.at[pl.ds(0, 15)], gains.at[pl.ds(0, 15)], once.at[8]).wait()

        @pl.loop(0, 16)
        def _(rel):
            rows = pl.ds(pl.multiple_of(rel * WIDTH, WIDTH), WIDTH)
            diagonal = lax.broadcasted_iota(jnp.int32, (WIDTH, WIDTH), 0) == lax.broadcasted_iota(
                jnp.int32, (WIDTH, WIDTH), 1
            )
            factor = jnp.sum(jnp.where(diagonal, gains[rel], 0.0), axis=1, keepdims=True)
            w_own[rows] = (w_own[rows].astype(jnp.float32) * factor).astype(jnp.bfloat16)
            w_sib[rows] = (w_sib[rows].astype(jnp.float32) * factor).astype(jnp.bfloat16)

    fold_gains()

    @pl.when(lax.rem(section, 2) == 1)
    def _():
        full_wait(relay_s, 18)
        for mask_x, mask_y in FAR + ((0, 0),):
            target = flipped(y, mask_y) * RING + flipped(x, mask_x)
            pltpu.make_async_remote_copy(
                src_ref=relay_s.at[target],
                dst_ref=widen_t.at[mp],
                send_sem=once.at[19],
                recv_sem=once.at[5],
                device_id=mesh_id(0, target * 2 + lax.div(section, 2)),
                device_id_type=MESH,
            ).start()

    @pl.when(section > 0)
    def _():
        spread(widen_s, widen_t, 4, 5)
        spread_own(widen_s, widen_t, 5)

    def adapter_of(index):
        return adapter_ref[lax.div(lax.rem(index, per_micro), BLOCK // CHUNK), lax.div(index, per_micro)]

    def first_sums(index):
        ring_slot = lax.rem(index, DEPTH)
        return [
            remote(
                sums_in.at[index, 0, 0, colour_rows(colour)],
                sums_in.at[index, 0, mask, colour_rows(colour)],
                as_.at[ring_slot, 0, colour, mask - 1],
                ar_.at[ring_slot, 0, colour, mask - 1],
                section,
                partner_of(colour, 0, mask),
            )
            for mask in (2, 3, 1)
            for colour in range(COLOURS)
        ]

    def second_rows(index):
        ring_slot = lax.rem(index, DEPTH)
        return [
            remote(
                gathered.at[index, colour, 0],
                gathered.at[index, colour, mask],
                gs.at[ring_slot, 1, colour, mask - 1],
                gr.at[ring_slot, 1, colour, mask - 1],
                section,
                partner_of(colour, 1, mask),
            )
            for mask in (3, 1)
            for colour in range(COLOURS)
        ]

    def third_rows(index):
        ring_slot = lax.rem(index, DEPTH)
        return [
            remote(
                gathered.at[index, colour, 4 - mask, pl.ds(half, 2)],
                gathered.at[index, colour, 2, pl.ds(half, 2)],
                ts.at[ring_slot, colour, half // 2],
                tr.at[ring_slot, colour, half // 2],
                section,
                partner_of(colour, 1, mask),
            )
            for mask, half in ((1, 0), (3, 2))
            for colour in range(COLOURS)
        ]

    def second_sums(index):
        ring_slot = lax.rem(index, DEPTH)
        return [
            remote(
                sums_out.at[index, colour_rows(colour)],
                sums_in.at[index, 1, mask, colour_rows(colour)],
                as_.at[ring_slot, 1, colour, mask - 1],
                ar_.at[ring_slot, 1, colour, mask - 1],
                section,
                partner_of(colour, 1, mask),
            )
            for mask in (2, 3, 1)
            for colour in range(COLOURS)
        ]

    def forward(index):
        for arriving, leaving in zip(second_rows(index), third_rows(index)):
            arriving.wait_recv()
            leaving.start()

    def relay(index):
        arriving, leaving = first_rows(index), second_rows(index)
        for colour in range(COLOURS):
            for copy in arriving[colour::COLOURS]:
                copy.wait_recv()
            for copy in leaving[colour::COLOURS]:
                copy.start()
        for copy in first_sums(index):
            copy.wait_recv()
        total = sums_in[index, 0, 0].astype(jnp.float32)
        for mask in (1, 2, 3):
            total = total + sums_in[index, 0, mask].astype(jnp.float32)
        running[index] = total
        sums_out[index] = total.astype(jnp.bfloat16)
        for copy in second_sums(index):
            copy.start()

    def finish_gather(index):
        for copy in second_sums(index) + third_rows(index):
            copy.wait_recv()
        total = running[index]
        for mask in (1, 2, 3):
            total = total + sums_in[index, 1, mask].astype(jnp.float32)
        rows = left_side(index).astype(jnp.float32)
        squares = jnp.sum(rows * rows, axis=1, keepdims=True)
        final_sums[index] = jnp.concatenate(
            [unpack(total), jnp.broadcast_to(squares, (CHUNK, LANES - RANK))], axis=1
        )

    def inner_products(h, scale_by, maps):
        scaled = (h.astype(jnp.float32) * scale_by).astype(jnp.bfloat16)
        inner = lax.dot_general(scaled, maps, (((1,), (1,)), ((), ())), preferred_element_type=jnp.float32)
        return pack(inner).astype(jnp.bfloat16)

    def own_rows(index):
        return jnp.concatenate([gathered[index, colour, 0, 0] for colour in range(COLOURS)], axis=0)

    def feed_sums(index):
        sums_in[index, 0, 0] = inner_products(own_rows(index), gain_o[...], narrow_t[adapter_of(index)])
        for copy in first_sums(index):
            copy.start()

    def left_side(index):
        return jnp.concatenate(
            [
                jnp.concatenate([gathered[(index, colour) + slot_of(colour, rel)] for colour in range(COLOURS)], axis=0)
                for rel in range(16)
            ],
            axis=1,
        )

    def swaps(index):
        ring_slot = lax.rem(index, DEPTH)
        sums = pltpu.make_async_remote_copy(
            src_ref=final_sums.at[index],
            dst_ref=sib_sums.at[index],
            send_sem=xs.at[ring_slot, 0],
            recv_sem=xr.at[ring_slot, 0],
            device_id=mesh_id(section, other),
            device_id_type=MESH,
        )
        parts = pltpu.make_async_remote_copy(
            src_ref=part_out.at[index],
            dst_ref=part_in.at[index],
            send_sem=xs.at[ring_slot, 1],
            recv_sem=xr.at[ring_slot, 1],
            device_id=mesh_id(section, other),
            device_id_type=MESH,
        )
        return sums, parts

    def multiply_sibling(index):
        sums, parts = swaps(index)
        sums.start()
        part_out[index] = jnp.dot(left_side(index), w_sib[...], preferred_element_type=jnp.float32)
        parts.start()

    def multiply_own(index):
        own_part[...] = jnp.dot(left_side(index), w_own[...], preferred_element_type=jnp.float32)

    def onward(index):
        ring_slot = lax.rem(index, DEPTH)
        return [
            remote(
                next_h.at[index, pl.ds(colour * PIECE, PIECE)],
                gathered.at[index, colour, 0, 0],
                zo.at[ring_slot, colour],
                zr.at[index, colour],
                section + 1,
                mp,
            )
            for colour in range(COLOURS)
        ]

    def homeward(index):
        home = lax.div(index, per_micro)
        part = lax.rem(index, per_micro)
        return pltpu.make_async_remote_copy(
            src_ref=next_h.at[index],
            dst_ref=finished.at[part],
            send_sem=zs.at[index],
            recv_sem=fr.at[part],
            device_id=mesh_id(home, mp),
            device_id_type=MESH,
        )

    def combine(index):
        sums, parts = swaps(index)
        sums.wait_recv()
        total = final_sums[index] + sib_sums[index]
        squares = total[:, RANK : RANK + 1]
        scale = lax.rsqrt(squares / (WIDTH * 32) + 1e-05)
        inner = total[:, :RANK].astype(jnp.bfloat16)
        delta = jnp.dot(inner, widen_t[adapter_of(index)], preferred_element_type=jnp.float32)
        own = own_part[...] + 2.0 * delta
        parts.wait_recv()
        base = own + part_in[index]
        leaving = onward(index)
        for colour in range(COLOURS):
            rows = slice(colour * PIECE, (colour + 1) * PIECE)
            h = gathered[index, colour, 0, 0].astype(jnp.float32)
            next_h[index, rows] = (h + scale[rows] * base[rows]).astype(jnp.bfloat16)

            @pl.when(section < 3)
            def _(colour=colour):
                leaving[colour].start()

        @pl.when(section == 3)
        def _():
            @pl.when(index < 3 * per_micro)
            def _():
                homeward(index).start()

            @pl.when(index >= 3 * per_micro)
            def _():
                part = lax.rem(index, per_micro)
                pltpu.make_async_copy(next_h.at[index], finished.at[part], fr.at[part]).start()

    def retire(index):
        for copy in first_rows(index) + first_sums(index) + second_rows(index) + second_sums(index) + third_rows(index):
            copy.wait_send()
        for copy in swaps(index):
            copy.wait_send()

        @pl.when(section < 3)
        def _():
            for copy in onward(index):
                copy.wait_send()

    full_wait(narrow_t, 7)

    @pl.loop(0, chunks + RETIRE)
    def _(tick):
        @pl.when(tick < chunks)
        def _():
            @pl.when((section > 0) | (tick >= EARLY))
            def _():
                feed_rows(tick)

            feed_sums(tick)

        @pl.when(tick == LATE)
        def _():
            part_wait(narrow_t, 6)
            full_wait(widen_t, 5)

            @pl.when(section > 0)
            def _():
                part_wait(widen_t, 4)

            @pl.when(lax.rem(section, 2) == 1)
            def _():
                full_wait(relay_s, 19)

            @pl.when(section == 0)
            def _():
                for half in (0, 1):
                    aside(half).wait_send()

        @pl.when((tick >= LATE) & (tick < chunks + LATE))
        def _():
            finish_gather(tick - LATE)
            multiply_sibling(tick - LATE)

        @pl.when((tick >= 1) & (tick <= chunks))
        def _():
            relay(tick - 1)

        @pl.when((tick >= LATE) & (tick < chunks + LATE))
        def _():
            multiply_own(tick - LATE)
            combine(tick - LATE)

        @pl.when((tick >= 2) & (tick <= chunks + 1))
        def _():
            forward(tick - 2)

        @pl.when(tick >= RETIRE)
        def _():
            retire(tick - RETIRE)

    @pl.when(section > 0)
    def _():
        for part in range(per_micro):
            for colour in range(COLOURS):
                piece = gathered.at[0, colour, 0, 0]
                pltpu.make_async_copy(piece, piece, fs.at[part, colour]).wait()

    @pl.when(section == 3)
    def _():
        @pl.loop(0, 3 * per_micro)
        def _(index):
            pltpu.make_async_copy(next_h.at[index], next_h.at[index], zs.at[index]).wait()

    for part in range(per_micro):
        pltpu.make_async_copy(finished.at[part], finished.at[part], fr.at[part]).wait()
    hidden = jnp.concatenate([finished[part] for part in range(per_micro)], axis=0)
    out_ref[...] = hidden
    head = jnp.broadcast_to(head_ref[...].reshape(1, WIDTH), (8, WIDTH))
    partial = lax.dot_general(head, hidden, (((1,), (1,)), ((), ())), preferred_element_type=jnp.float32)
    score_part[...] = partial[:1]

    for rank in plane_ranks:
        pltpu.make_async_remote_copy(
            src_ref=score_part,
            dst_ref=score_all.at[mp],
            send_sem=once.at[14],
            recv_sem=once.at[15],
            device_id=mesh_id(section, rank),
            device_id_type=MESH,
        ).start()

    pltpu.make_async_copy(score_part, score_all.at[mp], once.at[15]).start()
    pltpu.make_async_copy(score_all, score_all, once.at[15]).wait()
    pltpu.make_async_copy(score_all.at[pl.ds(0, 31)], score_all.at[pl.ds(0, 31)], once.at[14]).wait()
    raw = jnp.sum(score_all[...], axis=0)
    place = lax.broadcasted_iota(jnp.int32, (1, 2 * BLOCK), 1)
    limit = jnp.where(place < BLOCK, live_ref[0, 0], live_ref[0, 1])
    score_ref[...] = jnp.where(lax.rem(place, BLOCK) < limit, raw, 0.0)


def shards(
    entering_hidden,
    section_weight,
    section_norm_gain,
    plugin_narrowing_factors,
    plugin_widening_factors,
    reward_head,
    adapter_of_block,
    live_block_rows,
):
    chunks = 1024 // CHUNK
    bf16, f32 = jnp.bfloat16, jnp.float32
    vmem = pl.BlockSpec(memory_space=pltpu.VMEM)
    smem = pl.BlockSpec(memory_space=pltpu.SMEM)
    anywhere = pl.BlockSpec(memory_space=pl.ANY)
    dma = pltpu.SemaphoreType.DMA
    hidden, scores = pl.pallas_call(
        functools.partial(kernel, chunks),
        out_shape=(
            jax.ShapeDtypeStruct((256, WIDTH), bf16),
            jax.ShapeDtypeStruct((1, 256), f32),
        ),
        in_specs=[smem, smem, anywhere, anywhere, vmem, anywhere, anywhere, vmem],
        out_specs=(vmem, vmem),
        scratch_shapes=[
            pltpu.VMEM((chunks, COLOURS, RING, RING, PIECE, WIDTH), bf16),
            pltpu.VMEM((chunks, CHUNK // 2, LANES), bf16),
            pltpu.VMEM((chunks, PHASES, RING, CHUNK // 2, LANES), bf16),
            pltpu.VMEM((chunks, CHUNK // 2, LANES), f32),
            pltpu.VMEM((chunks, CHUNK, LANES), f32),
            pltpu.VMEM((chunks, CHUNK, LANES), f32),
            pltpu.VMEM((chunks, CHUNK, WIDTH), f32),
            pltpu.VMEM((chunks, CHUNK, WIDTH), f32),
            pltpu.VMEM((CHUNK, WIDTH), f32),
            pltpu.VMEM((chunks, CHUNK, WIDTH), bf16),
            pltpu.VMEM((16 * WIDTH, WIDTH), bf16),
            pltpu.VMEM((16 * WIDTH, WIDTH), bf16),
            pltpu.VMEM((32, RANK, WIDTH), bf16),
            pltpu.VMEM((32, RANK, WIDTH), bf16),
            pltpu.VMEM((16, RANK, WIDTH), bf16),
            pltpu.VMEM((32, RANK, WIDTH), bf16),
            pltpu.VMEM((32, RANK, WIDTH), bf16),
            pltpu.VMEM((1, WIDTH), f32),
            pltpu.VMEM((16, 1, WIDTH), f32),
            pltpu.VMEM((256 // CHUNK, CHUNK, WIDTH), bf16),
            pltpu.VMEM((1, 256), f32),
            pltpu.VMEM((32, 1, 256), f32),
            dma((DEPTH, PHASES, COLOURS, 3)),
            dma((DEPTH, PHASES, COLOURS, 3)),
            dma((DEPTH, PHASES, COLOURS, 3)),
            dma((DEPTH, PHASES, COLOURS, 3)),
            dma((DEPTH, COLOURS, 2)),
            dma((DEPTH, COLOURS, 2)),
            dma((DEPTH, 2)),
            dma((DEPTH, 2)),
            dma((chunks,)),
            dma((DEPTH, COLOURS)),
            dma((chunks, COLOURS)),
            dma((4, COLOURS)),
            dma((4,)),
            dma((20,)),
        ],
        compiler_params=pltpu.CompilerParams(
            collective_id=0, has_side_effects=True, vmem_limit_bytes=60 * 1024 * 1024
        ),
    )(
        adapter_of_block.T,
        live_block_rows,
        entering_hidden[0],
        section_weight[0],
        section_norm_gain,
        plugin_narrowing_factors[0, 0].T,
        plugin_widening_factors[0, 0],
        reward_head,
    )
    return hidden[None], scores


def solution(mesh):
    placed = (
        P("section", None, "mp"),
        P("section", None, "mp"),
        P("section", "mp"),
        P("section", "mp", None, None),
        P("section", "mp", None, None),
        P("mp"),
        P(),
        P("section", None),
    )
    return jax.shard_map(
        shards,
        mesh=mesh,
        in_specs=placed,
        out_specs=(P("section", None, "mp"), P("section", None)),
        check_vma=False,
    )
```
